512 devices in a mesh: dp: 16 (over z_hi, y), feat: 32 (over x, z_lo, core).
Axes of the slice: x: 4, y: 4, z: 16 (z_hi: 4, z_lo: 4; z = z_hi * 4 + z_lo), core: 2. Of those that a mesh axis runs over, the one named last changes fastest.
Arguments:
- sample: bfloat16 [16384, 2048], P(('dp', 'feat')), may hold values from -1800 to 1800
- pool: bfloat16 [32768, 2048], P(('dp', 'feat')), may hold values from -720 to 720
- old_min: float32 [32768], P(('dp', 'feat')), may hold values from 0.5 to 1.5
- centers: int32 [256], replicated, may hold values from 0 to 32767
Outputs:
- new_min: float32 [32768], P(('dp', 'feat'))
The draws below stay inside these ranges and needn't reach their ends.
All inputs are finite; a program needn't handle non-finite values.
Results may differ from the reference program's by a relative error of at most 0.00045.
Values may be sent and summed in bfloat16 or wider, within the bound.
A program may use at most 64 MiB of HBM per device.

```python
import math
import jax
import jax.numpy as jnp
from jax import lax

D = 2048
CENTERS = 256
ITERS = 2
SAMPLE = 16384
POOL = 32768


def column_scales(key):
    return jnp.exp(jax.random.uniform(jax.random.fold_in(key, 7), (D,), jnp.float32, 0.0, math.log(10.0)))


def draw_sample(key, part):
    scales = column_scales(key)
    noise_key, row_key = jax.random.split(jax.random.fold_in(key, 11))
    positions = jnp.arange(SAMPLE, dtype=jnp.float32) / SAMPLE
    values = jnp.clip(jax.random.normal(noise_key, (SAMPLE, D), jnp.float32), -6.0, 6.0)
    rising = 1.0 + 2.0 * positions
    row_scales = jnp.exp(jax.random.uniform(row_key, (SAMPLE, 1), jnp.float32, 0.0, math.log(10.0)))
    return (values * scales[None, :] * row_scales * rising[:, None]).astype(jnp.bfloat16)


def draw_pool(key, part):
    scales = column_scales(key)
    noise_key, row_key = jax.random.split(jax.random.fold_in(key, 13))
    values = jnp.clip(jax.random.normal(noise_key, (POOL, D), jnp.float32), -6.0, 6.0)
    row_scales = jnp.exp(jax.random.uniform(row_key, (POOL, 1), jnp.float32, math.log(6.0), math.log(12.0)))
    return (values * scales[None, :] * row_scales).astype(jnp.bfloat16)


def place_ends(result, key, smallest, largest):
    shape = result.shape
    place = [jax.random.randint(jax.random.fold_in(key, axis), (), 0, shape[axis]) for axis in range(len(shape))]
    result = result.at[tuple(place)].set(smallest)
    longest = shape.index(max(shape))
    place[longest] = (place[longest] + 1) % shape[longest]
    return result.at[tuple(place)].set(largest)


def level_of(key, extent, cuts, least, high):
    gain, own = 1.0, jax.random.fold_in(key, 6)
    for dim, parts in cuts:
        heights = jnp.exp(jax.random.uniform(jax.random.fold_in(own, dim), (parts,), jnp.float32, least / len(cuts), high / len(cuts)))
        gain = gain * jnp.repeat(heights, extent[dim] // parts).reshape([-1 if axis == dim else 1 for axis in range(len(extent))])
    return gain


def setup_inputs(seed: int = 0) -> dict:
    streams_of = jax.random.split(jax.random.key(seed), 5)
    sample = draw_sample(jax.random.fold_in(streams_of[4], 71), 0)
    pool = draw_pool(jax.random.fold_in(streams_of[4], 71), 0)
    old_min = jnp.clip(0.5 + 1.0 * jax.random.uniform(streams_of[2], (POOL,), jnp.float32) ** level_of(streams_of[2], (POOL,), ((0, 512),), -0.2, 0.2), 0.5, 1.5)
    centers = place_ends(jax.random.randint(streams_of[3], (CENTERS,), 0, POOL), jax.random.fold_in(streams_of[3], 1), 0, POOL - 1).astype(jnp.int32)
    return dict(sample=sample, pool=pool, old_min=old_min, centers=centers)


EPSILON = 1e-06

def newton_schulz(correlation):
    eye_matrix = jnp.eye(D, dtype=jnp.float32)
    highest = lax.Precision.HIGHEST
    current_y = correlation
    current_z = eye_matrix
    for turn_index in range(ITERS):
        if turn_index == 0:
            middle = current_y
        else:
            middle = jnp.dot(current_z, current_y, precision=highest)
        factor = 0.5 * (3.0 * eye_matrix - middle)
        if turn_index + 1 < ITERS:
            current_y = jnp.dot(current_y, factor, precision=highest)
        if turn_index == 0:
            current_z = factor
        else:
            current_z = jnp.dot(factor, current_z, precision=highest)
    return current_z

def reference(sample, pool, old_min, centers):
    sample_wide = sample.astype(jnp.float32)
    col_mean = lax.optimization_barrier(jnp.sum(sample_wide * sample_wide, axis=0)) / SAMPLE
    inverse = 1.0 / jnp.sqrt(col_mean + EPSILON)
    second = lax.dot_general(sample, sample, (((0,), (0,)), ((), ())), preferred_element_type=jnp.float32) / SAMPLE
    correlation = inverse[:, None] * second * inverse[None, :]
    root = newton_schulz(correlation)
    weights = (inverse[:, None] * root).astype(jnp.bfloat16)
    picked = jnp.dot(pool[centers], weights, preferred_element_type=jnp.float32).astype(jnp.bfloat16)
    picked_wide = picked.astype(jnp.float32)
    centre_norms = lax.optimization_barrier(jnp.sum(picked_wide * picked_wide, axis=1))
    block_rows = math.gcd(POOL, 4096)
    blocks = pool.reshape(POOL // block_rows, block_rows, D)

    def nearest_rows(row_block):
        whitened = jnp.dot(row_block, weights, preferred_element_type=jnp.float32).astype(jnp.bfloat16)
        whitened_wide = whitened.astype(jnp.float32)
        row_norms = lax.optimization_barrier(jnp.sum(whitened_wide * whitened_wide, axis=1))
        inner_products = lax.dot_general(whitened, picked, (((1,), (1,)), ((), ())), preferred_element_type=jnp.float32)
        squared = row_norms[:, None] + centre_norms[None, :] - 2.0 * inner_products
        return lax.optimization_barrier(jnp.min(jnp.maximum(squared, 0.0), axis=1)) / (2.0 * D)
    nearest_all = lax.map(nearest_rows, blocks).reshape(POOL)
    return jnp.minimum(old_min, nearest_all)
```

```python
import jax
import jax.numpy as jnp
from jax import lax
from jax.experimental import pallas as pl
from jax.experimental.pallas import tpu as pltpu
from jax.sharding import PartitionSpec as P

EPSILON = 1e-06
MESH = pl.DeviceIdType.MESH
F32 = jnp.float32
BF16 = jnp.bfloat16
LANES = 128
PANELS = 9
SLAB = 1536
GRAM = PANELS * LANES
DIAG = SLAB - LANES


def position():
    dp = lax.axis_index("dp")
    feat = lax.axis_index("feat")
    x, y = feat // 8, dp % 4
    z = (dp // 4) * 4 + (feat // 2) % 4
    return x, y, z, feat % 2


def device(x, y, z, core):
    return ((z // 4) * 4 + y, x * 8 + (z % 4) * 2 + core)


def greet(partners):
    barrier = pltpu.get_barrier_semaphore()
    for partner in partners:
        pl.semaphore_signal(barrier, inc=1, device_id=partner, device_id_type=MESH)
    pl.semaphore_wait(barrier, len(partners))


def remote(src, dst, send, recv, where):
    copy = pltpu.make_async_remote_copy(
        src_ref=src, dst_ref=dst, send_sem=send, recv_sem=recv, device_id=where, device_id_type=MESH
    )
    copy.start()
    return copy


def column_panels(chip):
    pair, half = chip // 2, chip % 2
    last = half if pair < 4 else 1 - half
    return [(2 * pair + step) % 16 for step in range(8)] + [(2 * pair + 8 + last) % 16]


def exchange_kernel(parcels, landed, send, recv, local):
    x, y, z, core = position()
    mine = x * 4 + y
    offsets = [(dx, dy) for dx in range(4) for dy in range(4) if dx or dy]
    greet([device((x + dx) % 4, (y + dy) % 4, z, core) for dx, dy in offsets])
    rows = pl.ds(pl.multiple_of(mine * 32, 32), 32)
    copies = []
    for slot, (dx, dy) in enumerate(offsets):
        to_x, to_y = (x + dx) % 4, (y + dy) % 4
        copies.append(
            remote(parcels.at[to_x * 4 + to_y], landed.at[:, rows, :], send.at[slot], recv.at[slot], device(to_x, to_y, z, core))
        )
    own = pltpu.make_async_copy(parcels.at[mine], landed.at[:, rows, :], local)
    own.start()
    own.wait()
    for copy in copies:
        copy.wait()


def gram_kernel(landed, chosen, partial):
    x, y, _, _ = position()
    half = y % 2
    left = landed[half]
    for step in range(PANELS):
        block = lax.dot_general(left, landed[step], (((0,), (0,)), ((), ())), preferred_element_type=F32)
        if step < 2:
            rows = lax.broadcasted_iota(jnp.int32, block.shape, 0)
            cols = lax.broadcasted_iota(jnp.int32, block.shape, 1)
            block = jnp.where((rows == cols) & (half == step), 0.0, block)
        lanes = slice(step * LANES, (step + 1) * LANES)
        partial[0, :, lanes] = block[:64]
        partial[1, :, lanes] = block[64:]
    picked = jnp.zeros((256, LANES), F32)
    for part in range(2):
        picked += jnp.dot(chosen[part], landed[PANELS + part], preferred_element_type=F32)
    for part in range(4):
        lanes = slice(GRAM + (part % 2) * LANES, GRAM + (part % 2 + 1) * LANES)
        partial[part // 2, :, lanes] = picked[part * 64 : part * 64 + 64]
    wide = left.astype(F32)
    squares = jnp.sum(wide * wide, axis=0, keepdims=True)
    first = lax.broadcasted_iota(jnp.int32, (64, LANES), 0) == 0
    for core in range(2):
        partial[core, :, DIAG:] = jnp.where(first, squares, 0.0)


def in_three(total):
    high = total.astype(BF16).astype(F32)
    middle = (total - high).astype(BF16).astype(F32)
    low = total - high - middle
    rows = lax.broadcasted_iota(jnp.int32, (16, LANES), 0)
    return jnp.where(rows == 0, high, jnp.where(rows == 1, middle, jnp.where(rows == 2, low, 0.0)))


def reduce_kernel(partial, summed, other, mine, terms, chunk, core_send, core_recv, send, recv, send_back, recv_back):
    x, y, z, core = position()
    column = [(z + offset) % 16 for offset in range(16)]
    greet([device(x, y, z, 1 - core)] + [device(x, y, k, core) for k in column[1:]])
    remote(partial.at[1 - core], other, core_send, core_recv, device(x, y, z, 1 - core)).wait()
    mine[:, :DIAG] = (partial[core, :, :DIAG] + other[:, :DIAG]).astype(BF16)
    squares = partial[core, 0:1, DIAG:] + other[0:1, DIAG:]
    mine[0:16, DIAG:] = in_three(squares).astype(BF16)
    mine[16:64, DIAG:] = jnp.zeros((48, LANES), BF16)

    def part_of(ref, k):
        return ref.at[pl.ds(pl.multiple_of((k // 4) * 16, 16), 16), pl.ds(pl.multiple_of((k % 4) * 384, 384), 384)]

    copies = [
        remote(part_of(mine, column[o]), terms.at[o], send.at[o], recv.at[o], device(x, y, column[o], core))
        for o in range(1, 16)
    ]
    total = part_of(mine, z)[...].astype(F32)
    for o in range(1, 16):
        copies[o - 1].wait()
        total += terms[o].astype(F32)
    squares = total[0:1, 256:] + total[1:2, 256:] + total[2:3, 256:]
    chunk[:, :256] = total[:, :256].astype(BF16)
    chunk[:, 256:] = jnp.where(z == 3, in_three(squares), total[:, 256:]).astype(BF16)
    copies = [
        remote(chunk, part_of(summed, z), send_back.at[o], recv_back.at[o], device(x, y, column[o], core))
        for o in range(1, 16)
    ]
    part_of(summed, z)[...] = chunk[...]
    for copy in copies:
        copy.wait()


def spread_kernel(slab, everything, send, recv, local):
    x, y, z, core = position()
    twin = device(x, y, z, 1 - core)
    across_x = [(x + d) % 4 for d in range(4)]
    across_y = [(y + d) % 4 for d in range(4)]
    from_x = [(x + 4 - d) % 4 for d in range(4)]
    from_y = [(y + 4 - d) % 4 for d in range(4)]
    greet(
        [twin]
        + [device(across_x[d], y, z, core) for d in range(1, 4)]
        + [device(x, across_y[d], z, core) for d in range(1, 4)]
    )
    upper, lower = pl.ds(0, 32), pl.ds(32, 32)
    own = pltpu.make_async_copy(slab, everything.at[x, y, core], local)
    own.start()
    slot = iter(range(25))

    def go(src, dst, where):
        n = next(slot)
        return remote(src, dst, send.at[n], recv.at[n], where)

    first_x, first_y = [], []
    for d in range(1, 4):
        first_x.append(go(slab.at[upper], everything.at[x, y, core, upper], device(across_x[d], y, z, core)))
        first_y.append(go(slab.at[lower], everything.at[x, y, core, lower], device(x, across_y[d], z, core)))
    rest = [go(slab, everything.at[x, y, core], twin)]
    own.wait()
    for copy in first_x:
        copy.wait()
    second_y = []
    block = everything.at[:, y, core, upper]
    for d in range(1, 4):
        second_y.append(go(block, block, device(x, across_y[d], z, core)))
    for copy in first_y:
        copy.wait()
    second_x = []
    block = everything.at[x, :, core, lower]
    for d in range(1, 4):
        second_x.append(go(block, block, device(across_x[d], y, z, core)))
    for d in range(1, 4):
        block = everything.at[from_x[d], y, core, upper]
        rest.append(go(block, block, twin))
        block = everything.at[x, from_y[d], core, lower]
        rest.append(go(block, block, twin))
    for d in range(1, 4):
        second_y[d - 1].wait()
        block = everything.at[:, from_y[d], core, upper]
        rest.append(go(block, block, twin))
        second_x[d - 1].wait()
        block = everything.at[from_x[d], :, core, lower]
        rest.append(go(block, block, twin))
    for copy in rest:
        copy.wait()


def whiten_kernel(sample_total, blocks, pool, whitened, start, held, ready, corner, scale, extra):
    count = start.shape[0]
    for chip in range(16):
        lanes = slice(chip * LANES, (chip + 1) * LANES)
        parts = blocks[chip * LANES : chip * LANES + 16, DIAG:].astype(F32)
        mean = (parts[0:1] + parts[1:2] + parts[2:3]) / sample_total
        inverse = 1.0 / jnp.sqrt(mean + EPSILON)
        scale[0:1, lanes] = inverse
        extra[0:1, lanes] = inverse * mean * inverse - 1.0
        for part in range(4):
            rows = slice(chip * LANES + (part // 2) * 64, chip * LANES + (part // 2) * 64 + 64)
            source = slice(GRAM + (part % 2) * LANES, GRAM + (part % 2 + 1) * LANES)
            start[part * 64 : part * 64 + 64, lanes] = blocks[rows, source].astype(F32) * inverse
        start[256:, lanes] = pool[:, lanes].astype(F32) * inverse
    for pair in range(4):
        for half in range(2):
            rows = slice(half * LANES, (half + 1) * LANES)
            others = slice((1 - half) * LANES, (2 - half) * LANES)
            top = (2 * pair + half) * LANES
            corner[pair, rows, rows] = blocks[top : top + LANES, GRAM - LANES : GRAM]
            top = (2 * pair + 8 + half) * LANES
            corner[pair, others, rows] = blocks[top : top + LANES, GRAM - LANES : GRAM].astype(F32).T.astype(BF16)
    held[...] = start[...] * (1.0 / 16.0)

    def transposed(left, right):
        return lax.dot_general(left, right, (((1,), (1,)), ((), ())), preferred_element_type=F32)

    @pl.loop(0, 4)
    def _(turn):
        factor = jnp.where(turn == 0, -0.3125, jnp.where(turn == 1, 0.375, jnp.where(turn == 2, -0.5, 1.0)))
        for j in range(8):
            lanes = slice(j * 256, (j + 1) * 256)
            scaled = (held[:, lanes] * scale[0:1, lanes]).astype(BF16)
            ready[:, lanes] = scaled
            if j < 3:
                ready[:, 2048 + j * 256 : 2048 + (j + 1) * 256] = scaled
        for j in range(8):
            lanes = slice(j * 256, (j + 1) * 256)
            out = transposed(ready[:, (j + 1) * 256 : (j + 4) * 256], blocks[lanes, 256:1024])
            for d in range(4):
                i = (j - d) % 8
                out += jnp.dot(
                    ready[:, i * 256 : (i + 1) * 256],
                    blocks[i * 256 : (i + 1) * 256, d * 256 : (d + 1) * 256],
                    preferred_element_type=F32,
                )
            if j >= 4:
                out += jnp.dot(ready[:, (j - 4) * 256 : (j - 3) * 256], corner[j - 4], preferred_element_type=F32)
            else:
                out += transposed(ready[:, (j + 4) * 256 : (j + 5) * 256], corner[j])
            held[:, lanes] = (
                out * (scale[0:1, lanes] * (1.0 / sample_total))
                + held[:, lanes] * extra[0:1, lanes]
                + factor * start[:, lanes]
            )

    whitened[...] = held[...].astype(BF16)


VMEM = pl.BlockSpec(memory_space=pltpu.VMEM)
DMA = pltpu.SemaphoreType.DMA


def parameters(collective=None, limit=48):
    if collective is None:
        return pltpu.CompilerParams(vmem_limit_bytes=limit * 1024 * 1024)
    return pltpu.CompilerParams(collective_id=collective, has_side_effects=True, vmem_limit_bytes=limit * 1024 * 1024)


def squared_terms(row_values, centre_rows):
    row_wide = row_values.astype(F32)
    centre_wide = centre_rows.astype(F32)
    row_norms = jnp.sum(row_wide * row_wide, axis=1)
    centre_norms = jnp.sum(centre_wide * centre_wide, axis=1)
    inner_products = lax.dot_general(row_values, centre_rows, (((1,), (1,)), ((), ())), preferred_element_type=F32)
    return row_norms[:, None] + centre_norms[None, :] - 2.0 * inner_products


def per_device(sample, pool, old_min, centers):
    width = sample.shape[1]
    pool_count = pool.shape[0]
    sample_total = sample.shape[0] * lax.axis_size("dp") * lax.axis_size("feat")
    x, y, z, core = position()
    sample_panels = sample.reshape(32, 16, LANES).transpose(1, 0, 2)
    pool_panels = pool.reshape(2, 32, 16, LANES).transpose(2, 0, 1, 3)
    parcels = jnp.stack(
        [
            jnp.concatenate([sample_panels[k : k + 1] for k in column_panels(chip)] + [pool_panels[chip]], axis=0)
            for chip in range(16)
        ]
    )
    landed = pl.pallas_call(
        exchange_kernel,
        out_shape=jax.ShapeDtypeStruct((PANELS + 2, 512, LANES), BF16),
        in_specs=[VMEM],
        out_specs=VMEM,
        scratch_shapes=[DMA((15,)), DMA((15,)), DMA],
        compiler_params=parameters(0),
    )(parcels)
    chips = jnp.arange(16, dtype=jnp.int32)
    owners = ((z // 4) * 4 + chips % 4) * 32 + (chips // 4) * 8 + (z % 4) * 2 + core
    row_ids = (
        owners[None, :, None] * pool_count
        + jnp.arange(2, dtype=jnp.int32)[:, None, None] * 32
        + jnp.arange(32, dtype=jnp.int32)[None, None, :]
    ).reshape(2, 512)
    chosen = (centers[None, :, None] == row_ids[:, None, :]).astype(BF16)
    partial = pl.pallas_call(
        gram_kernel,
        out_shape=jax.ShapeDtypeStruct((2, 64, SLAB), F32),
        in_specs=[VMEM, VMEM],
        out_specs=VMEM,
        compiler_params=parameters(),
    )(landed, chosen)
    summed = pl.pallas_call(
        reduce_kernel,
        out_shape=jax.ShapeDtypeStruct((64, SLAB), BF16),
        in_specs=[VMEM],
        out_specs=VMEM,
        scratch_shapes=[
            pltpu.VMEM((64, SLAB), F32),
            pltpu.VMEM((64, SLAB), BF16),
            pltpu.VMEM((16, 16, 384), BF16),
            pltpu.VMEM((16, 384), BF16),
            DMA,
            DMA,
            DMA((16,)),
            DMA((16,)),
            DMA((16,)),
            DMA((16,)),
        ],
        compiler_params=parameters(1),
    )(partial)
    everything = pl.pallas_call(
        spread_kernel,
        out_shape=jax.ShapeDtypeStruct((4, 4, 2, 64, SLAB), BF16),
        in_specs=[VMEM],
        out_specs=VMEM,
        scratch_shapes=[DMA((25,)), DMA((25,)), DMA],
        compiler_params=parameters(2),
    )(summed)
    count = 256 + pool_count
    whitened = pl.pallas_call(
        lambda *refs: whiten_kernel(float(sample_total), *refs),
        out_shape=jax.ShapeDtypeStruct((count, width), BF16),
        in_specs=[VMEM, VMEM],
        out_specs=VMEM,
        scratch_shapes=[
            pltpu.VMEM((count, width), F32),
            pltpu.VMEM((count, width), F32),
            pltpu.VMEM((count, width + 768), BF16),
            pltpu.VMEM((4, 256, 256), BF16),
            pltpu.VMEM((8, width), F32),
            pltpu.VMEM((8, width), F32),
        ],
        compiler_params=parameters(),
    )(everything.reshape(width, SLAB), pool)
    squared = squared_terms(whitened[256:], whitened[:256])
    nearest = jnp.min(jnp.maximum(squared, 0.0), axis=1) / (2.0 * width)
    return jnp.minimum(old_min, nearest)


def solution(mesh):
    return jax.shard_map(
        per_device,
        mesh=mesh,
        in_specs=(P(("dp", "feat"), None), P(("dp", "feat"), None), P(("dp", "feat")), P()),
        out_specs=P(("dp", "feat")),
        check_vma=False,
    )
```

```python
import jax
import jax.numpy as jnp
from jax import lax
from jax.experimental import pallas as pl
from jax.experimental.pallas import tpu as pltpu
from jax.sharding import PartitionSpec as P

EPSILON = 1e-06
MESH = pl.DeviceIdType.MESH
F32 = jnp.float32
BF16 = jnp.bfloat16
LANES = 128
PANELS = 9
SLAB = 1536
GRAM = PANELS * LANES
DIAG = SLAB - LANES


def position():
    dp = lax.axis_index("dp")
    feat = lax.axis_index("feat")
    x, y = feat // 8, dp % 4
    z = (dp // 4) * 4 + (feat // 2) % 4
    return x, y, z, feat % 2


def device(x, y, z, core):
    return ((z // 4) * 4 + y, x * 8 + (z % 4) * 2 + core)


def remote(src, dst, send, recv, where):
    copy = pltpu.make_async_remote_copy(
        src_ref=src, dst_ref=dst, send_sem=send, recv_sem=recv, device_id=where, device_id_type=MESH
    )
    copy.start()
    return copy


def column_panels(chip):
    pair, half = chip // 2, chip % 2
    last = half if pair < 4 else 1 - half
    return [(2 * pair + step) % 16 for step in range(8)] + [(2 * pair + 8 + last) % 16]


def in_three(total):
    high = total.astype(BF16).astype(F32)
    middle = (total - high).astype(BF16).astype(F32)
    low = total - high - middle
    rows = lax.broadcasted_iota(jnp.int32, (16, LANES), 0)
    return jnp.where(rows == 0, high, jnp.where(rows == 1, middle, jnp.where(rows == 2, low, 0.0)))


def rows_dot(left, right):
    return lax.dot_general(left, right, (((0,), (0,)), ((), ())), preferred_element_type=F32)


def tiles(ref, k):
    return ref.at[pl.ds(pl.multiple_of((k // 4) * 16, 16), 16), pl.ds(pl.multiple_of((k % 4) * 384, 384), 384)]


def moments_kernel(
    sample, pool, centers, everything, parcels, landed, partial, other, mine, terms, chunk, local, plane_send, plane_recv,
    core_send, core_recv, send, recv, send_back, recv_back, piece_send, piece_recv,
):
    x, y, z, core = position()
    here = x * 4 + y
    twin = device(x, y, z, 1 - core)
    column = [(z + o) % 16 for o in range(16)]
    offsets = [(dx, dy) for dx in range(4) for dy in range(4) if dx or dy]
    barrier = pltpu.get_barrier_semaphore()
    partners = [device(x, y, column[(8 + o // 2 if o % 2 else 8 - o // 2)], core) for o in range(1, 16)]
    partners += [device((x + dx) % 4, (y + dy) % 4, z, core) for dx, dy in offsets] + [twin]
    for partner in partners:
        pl.semaphore_signal(barrier, inc=1, device_id=partner, device_id_type=MESH)

    for chip in range(16):
        for step, panel in enumerate(column_panels(chip)):
            parcels[chip, step] = sample[:, panel * LANES : (panel + 1) * LANES]
        for part in range(2):
            parcels[chip, PANELS + part] = pool[part * 32 : part * 32 + 32, chip * LANES : (chip + 1) * LANES]
    pl.semaphore_wait(barrier, len(partners))

    rows = pl.ds(pl.multiple_of(here * 32, 32), 32)
    copies = []
    for slot, (dx, dy) in enumerate(offsets):
        to_x, to_y = (x + dx) % 4, (y + dy) % 4
        copies.append(
            remote(parcels.at[to_x * 4 + to_y], landed.at[:, rows, :], plane_send.at[slot], plane_recv.at[slot], device(to_x, to_y, z, core))
        )
    own = pltpu.make_async_copy(parcels.at[here], landed.at[:, rows, :], local)
    own.start()
    row = lax.broadcasted_iota(jnp.int32, (512, 256), 0)
    owner = ((z // 4) * 4 + ((row >> 5) & 3)) * 32 + (row >> 7) * 8 + (z % 4) * 2 + core
    row_id = owner * 64 + (row & 31)
    chosen = [jnp.where(row_id + part * 32 == centers[...], 1.0, 0.0).astype(BF16) for part in range(2)]
    own.wait()
    for copy in copies:
        copy.wait()

    half = y % 2
    left = landed[half]
    for step in range(PANELS):
        block = rows_dot(left, landed[step])
        if step < 2:
            down = lax.broadcasted_iota(jnp.int32, block.shape, 0)
            along = lax.broadcasted_iota(jnp.int32, block.shape, 1)
            block = jnp.where((down == along) & (half == step), 0.0, block)
        lanes = slice(step * LANES, (step + 1) * LANES)
        partial[0, :, lanes] = block[:64]
        partial[1, :, lanes] = block[64:]
    picked = rows_dot(chosen[0], landed[PANELS]) + rows_dot(chosen[1], landed[PANELS + 1])
    for part in range(4):
        lanes = slice(GRAM + (part % 2) * LANES, GRAM + (part % 2 + 1) * LANES)
        partial[part // 2, :, lanes] = picked[part * 64 : part * 64 + 64]
    wide = left.astype(F32)
    squares = jnp.sum(wide * wide, axis=0, keepdims=True)
    first = lax.broadcasted_iota(jnp.int32, (64, LANES), 0) == 0
    for side in range(2):
        partial[side, :, DIAG:] = jnp.where(first, squares, 0.0)

    remote(partial.at[1 - core], other, core_send, core_recv, twin).wait()
    mine[:, :DIAG] = (partial[core, :, :DIAG] + other[:, :DIAG]).astype(BF16)
    squares = partial[core, 0:1, DIAG:] + other[0:1, DIAG:]
    mine[0:16, DIAG:] = in_three(squares).astype(BF16)
    mine[16:64, DIAG:] = jnp.zeros((48, LANES), BF16)

    far_first = [8] + [o for d in range(7, 0, -1) for o in (d, 16 - d)]
    copies = {
        o: remote(tiles(mine, column[o]), terms.at[o], send.at[o], recv.at[o], device(x, y, column[o], core)) for o in far_first
    }
    total = tiles(mine, z)[...].astype(F32)
    for o in reversed(far_first):
        copies[o].wait()
        total += terms[o].astype(F32)
    squares = total[0:1, 256:] + total[1:2, 256:] + total[2:3, 256:]
    chunk[:, :256] = total[:, :256].astype(BF16)
    chunk[:, 256:] = jnp.where(z == 3, in_three(squares), total[:, 256:]).astype(BF16)

    slab = everything.at[x, y, core]
    tiles(slab, z)[...] = chunk[...]
    back = {
        o: remote(chunk, tiles(slab, z), send_back.at[o], recv_back.at[z], device(x, y, column[o], core)) for o in far_first
    }
    pending = list(back.values())

    def gathered(k):
        pltpu.make_async_remote_copy(
            src_ref=chunk, dst_ref=tiles(slab, k), send_sem=send_back.at[0], recv_sem=recv_back.at[k], device_id=twin, device_id_type=MESH
        ).wait_recv()

    zone = z // 4
    counter = iter(range(200))

    class Strip:
        def __init__(self, shift, flip, sign):
            self.a = (zone + shift) % 4
            self.shift, self.flip, self.sign = shift, flip, sign
            self.rows = pl.ds(pl.multiple_of(self.a * 16, 16), 16)
            p, q = (y, x) if flip else (x, y)
            self.p = [p, (p + 4 - sign) % 4, (p + 4 + sign) % 4, (p + 2) % 4]
            self.q = [q, (q + 4 - sign) % 4, (q + 4 + sign) % 4, (q + 2) % 4]
            self.ahead, self.behind = [], []
            self.onward = []

        def where(self, p, q):
            return device(q, p, z, core) if self.flip else device(p, q, z, core)

        def piece(self, p, q):
            return everything.at[q, p, core, self.rows] if self.flip else everything.at[p, q, core, self.rows]

        def line(self, q):
            return everything.at[q, :, core, self.rows] if self.flip else everything.at[:, q, core, self.rows]

        def go(self, ref, target):
            n = next(counter)
            copy = remote(ref, ref, piece_send.at[n], piece_recv.at[n], target)
            pending.append(copy)
            return copy

        def across(self, n):
            piece = self.piece(self.p[n], self.q[0])
            self.ahead.append(self.go(piece, self.where(self.p[0], self.q[2])))
            self.behind.append(self.go(piece, self.where(self.p[0], self.q[1])))

        def begin(self):
            if self.shift == 0:
                for step in range(1, 4):
                    gathered(zone * 4 + (z + step) % 4)
            else:
                for step in range(4):
                    gathered(self.a * 4 + step)
            piece = self.piece(self.p[0], self.q[0])
            self.up = self.go(piece, self.where(self.p[2], self.q[0]))
            self.down = self.go(piece, self.where(self.p[1], self.q[0]))
            self.across(0)

        def second(self):
            self.up.wait_recv()
            self.far = self.go(self.piece(self.p[1], self.q[0]), self.where(self.p[2], self.q[0]))
            self.across(1)
            self.down.wait_recv()
            self.across(2)

        def third(self):
            self.far.wait_recv()
            self.across(3)
            self.twins = [self.go(self.line(self.q[0]), twin)]

        def fourth(self):
            for n in range(4):
                self.ahead[n].wait_recv()
                self.onward.append(self.go(self.piece(self.p[n], self.q[1]), self.where(self.p[0], self.q[2])))
            self.twins.append(self.go(self.line(self.q[1]), twin))
            for n in range(4):
                self.behind[n].wait_recv()
            self.twins.append(self.go(self.line(self.q[2]), twin))

        def fifth(self):
            for copy in self.onward:
                copy.wait_recv()
            self.twins.append(self.go(self.line(self.q[3]), twin))

        def last(self):
            for copy in self.twins:
                copy.wait_recv()

    s0, s1, s2, s3 = Strip(0, False, 1), Strip(1, True, 1), Strip(3, False, -1), Strip(2, True, -1)
    s0.begin(), s1.begin(), s2.begin()
    s0.second(), s1.second(), s3.begin(), s2.second()
    s0.third(), s1.third(), s3.second(), s2.third()
    s0.fourth(), s1.fourth(), s3.third(), s2.fourth()
    s0.fifth(), s1.fifth(), s3.fourth(), s2.fifth(), s3.fifth()
    for strip in (s0, s1, s2, s3):
        strip.last()
    for copy in pending:
        copy.wait_send()


def whiten_kernel(sample_total, blocks, pool, whitened, start, held, ready, corner, scale, extra):
    count = start.shape[0]
    for chip in range(16):
        lanes = slice(chip * LANES, (chip + 1) * LANES)
        parts = blocks[chip * LANES : chip * LANES + 16, DIAG:].astype(F32)
        mean = (parts[0:1] + parts[1:2] + parts[2:3]) / sample_total
        inverse = 1.0 / jnp.sqrt(mean + EPSILON)
        scale[0:1, lanes] = inverse
        extra[0:1, lanes] = inverse * mean * inverse - 1.0
        for part in range(4):
            rows = slice(chip * LANES + (part // 2) * 64, chip * LANES + (part // 2) * 64 + 64)
            source = slice(GRAM + (part % 2) * LANES, GRAM + (part % 2 + 1) * LANES)
            start[part * 64 : part * 64 + 64, lanes] = blocks[rows, source].astype(F32) * inverse
        start[256:, lanes] = pool[:, lanes].astype(F32) * inverse
    for pair in range(4):
        for half in range(2):
            rows = slice(half * LANES, (half + 1) * LANES)
            others = slice((1 - half) * LANES, (2 - half) * LANES)
            top = (2 * pair + half) * LANES
            corner[pair, rows, rows] = blocks[top : top + LANES, GRAM - LANES : GRAM]
            top = (2 * pair + 8 + half) * LANES
            corner[pair, others, rows] = blocks[top : top + LANES, GRAM - LANES : GRAM].astype(F32).T.astype(BF16)
    held[...] = start[...] * (1.0 / 16.0)

    def transposed(left, right):
        return lax.dot_general(left, right, (((1,), (1,)), ((), ())), preferred_element_type=F32)

    @pl.loop(0, 4)
    def _(turn):
        factor = jnp.where(turn == 0, -0.3125, jnp.where(turn == 1, 0.375, jnp.where(turn == 2, -0.5, 1.0)))
        for j in range(8):
            lanes = slice(j * 256, (j + 1) * 256)
            scaled = (held[:, lanes] * scale[0:1, lanes]).astype(BF16)
            ready[:, lanes] = scaled
            if j < 3:
                ready[:, 2048 + j * 256 : 2048 + (j + 1) * 256] = scaled
        for j in range(8):
            lanes = slice(j * 256, (j + 1) * 256)
            out = transposed(ready[:, (j + 1) * 256 : (j + 4) * 256], blocks[lanes, 256:1024])
            for d in range(4):
                i = (j - d) % 8
                out += jnp.dot(
                    ready[:, i * 256 : (i + 1) * 256],
                    blocks[i * 256 : (i + 1) * 256, d * 256 : (d + 1) * 256],
                    preferred_element_type=F32,
                )
            if j >= 4:
                out += jnp.dot(ready[:, (j - 4) * 256 : (j - 3) * 256], corner[j - 4], preferred_element_type=F32)
            else:
                out += transposed(ready[:, (j + 4) * 256 : (j + 5) * 256], corner[j])
            held[:, lanes] = (
                out * (scale[0:1, lanes] * (1.0 / sample_total))
                + held[:, lanes] * extra[0:1, lanes]
                + factor * start[:, lanes]
            )

    whitened[...] = held[...].astype(BF16)


VMEM = pl.BlockSpec(memory_space=pltpu.VMEM)
DMA = pltpu.SemaphoreType.DMA


def parameters(collective=None, limit=48):
    if collective is None:
        return pltpu.CompilerParams(vmem_limit_bytes=limit * 1024 * 1024)
    return pltpu.CompilerParams(collective_id=collective, has_side_effects=True, vmem_limit_bytes=limit * 1024 * 1024)


def squared_terms(row_values, centre_rows):
    row_wide = row_values.astype(F32)
    centre_wide = centre_rows.astype(F32)
    row_norms = jnp.sum(row_wide * row_wide, axis=1)
    centre_norms = jnp.sum(centre_wide * centre_wide, axis=1)
    inner_products = lax.dot_general(row_values, centre_rows, (((1,), (1,)), ((), ())), preferred_element_type=F32)
    return row_norms[:, None] + centre_norms[None, :] - 2.0 * inner_products


def per_device(sample, pool, old_min, centers):
    width = sample.shape[1]
    pool_count = pool.shape[0]
    sample_total = sample.shape[0] * lax.axis_size("dp") * lax.axis_size("feat")
    everything = pl.pallas_call(
        moments_kernel,
        out_shape=jax.ShapeDtypeStruct((4, 4, 2, 64, SLAB), BF16),
        in_specs=[VMEM, VMEM, VMEM],
        out_specs=VMEM,
        scratch_shapes=[
            pltpu.VMEM((16, PANELS + 2, 32, LANES), BF16),
            pltpu.VMEM((PANELS + 2, 512, LANES), BF16),
            pltpu.VMEM((2, 64, SLAB), F32),
            pltpu.VMEM((64, SLAB), F32),
            pltpu.VMEM((64, SLAB), BF16),
            pltpu.VMEM((16, 16, 384), BF16),
            pltpu.VMEM((16, 384), BF16),
            DMA,
            DMA((15,)),
            DMA((15,)),
            DMA,
            DMA,
            DMA((16,)),
            DMA((16,)),
            DMA((16,)),
            DMA((16,)),
            DMA((76,)),
            DMA((76,)),
        ],
        compiler_params=parameters(0, 16),
    )(sample, pool, centers.reshape(1, 256))
    count = 256 + pool_count
    whitened = pl.pallas_call(
        lambda *refs: whiten_kernel(float(sample_total), *refs),
        out_shape=jax.ShapeDtypeStruct((count, width), BF16),
        in_specs=[VMEM, VMEM],
        out_specs=VMEM,
        scratch_shapes=[
            pltpu.VMEM((count, width), F32),
            pltpu.VMEM((count, width), F32),
            pltpu.VMEM((count, width + 768), BF16),
            pltpu.VMEM((4, 256, 256), BF16),
            pltpu.VMEM((8, width), F32),
            pltpu.VMEM((8, width), F32),
        ],
        compiler_params=parameters(None, 24),
    )(everything.reshape(width, SLAB), pool)
    squared = squared_terms(whitened[256:], whitened[:256])
    nearest = jnp.min(jnp.maximum(squared, 0.0), axis=1) / (2.0 * width)
    return jnp.minimum(old_min, nearest)


def solution(mesh):
    return jax.shard_map(
        per_device,
        mesh=mesh,
        in_specs=(P(("dp", "feat"), None), P(("dp", "feat"), None), P(("dp", "feat")), P()),
        out_specs=P(("dp", "feat")),
        check_vma=False,
    )
```

```python
import jax
import jax.numpy as jnp
from jax import lax
from jax.experimental import pallas as pl
from jax.experimental.pallas import tpu as pltpu
from jax.sharding import PartitionSpec as P

EPSILON = 1e-06
MESH = pl.DeviceIdType.MESH
F32 = jnp.float32
BF16 = jnp.bfloat16
LANES = 128
PANELS = 9
SLAB = 1536
GRAM = PANELS * LANES
DIAG = SLAB - LANES


def position():
    dp = lax.axis_index("dp")
    feat = lax.axis_index("feat")
    x, y = feat // 8, dp % 4
    z = (dp // 4) * 4 + (feat // 2) % 4
    return x, y, z, feat % 2


def device(x, y, z, core):
    return ((z // 4) * 4 + y, x * 8 + (z % 4) * 2 + core)


def remote(src, dst, send, recv, where):
    copy = pltpu.make_async_remote_copy(
        src_ref=src, dst_ref=dst, send_sem=send, recv_sem=recv, device_id=where, device_id_type=MESH
    )
    copy.start()
    return copy


def column_panels(chip):
    pair, half = chip // 2, chip % 2
    last = half if pair < 4 else 1 - half
    return [(2 * pair + step) % 16 for step in range(8)] + [(2 * pair + 8 + last) % 16]


def in_three(total, count):
    high = total.astype(BF16).astype(F32)
    middle = (total - high).astype(BF16).astype(F32)
    low = total - high - middle
    rows = lax.broadcasted_iota(jnp.int32, (count, LANES), 0)
    return jnp.where(rows == 0, high, jnp.where(rows == 1, middle, jnp.where(rows == 2, low, 0.0)))


def rows_dot(left, right):
    return lax.dot_general(left, right, (((0,), (0,)), ((), ())), preferred_element_type=F32)


def moments_kernel(
    sample_in, pool_in, centers, everything, sample, pool, parcels_a, parcels_b, landed_a, landed_b, partial, other, mine, terms,
    chunk, local, plane_send, plane_recv, core_send, core_recv, send, recv, send_back, recv_back, piece_send, piece_recv,
):
    x, y, z, core = position()
    here = x * 4 + y
    twin = device(x, y, z, 1 - core)
    column = [(z + o) % 16 for o in range(16)]
    far_first = [8] + [o for d in range(7, 0, -1) for o in (d, 16 - d)]
    offsets = [(dx, dy) for dx in range(4) for dy in range(4) if dx or dy]
    loads = [
        pltpu.make_async_copy(sample_in, sample, local.at[0]),
        pltpu.make_async_copy(pool_in, pool, local.at[1]),
    ]
    for copy in loads:
        copy.start()
    barrier = pltpu.get_barrier_semaphore()
    partners = [device(x, y, column[o], core) for o in far_first]
    partners += [device((x + dx) % 4, (y + dy) % 4, z, core) for dx, dy in offsets] + [twin]
    for partner in partners:
        pl.semaphore_signal(barrier, inc=1, device_id=partner, device_id_type=MESH)

    for copy in loads:
        copy.wait()
    for chip in range(16):
        for step, panel in enumerate(column_panels(chip)):
            block = sample[:, panel * LANES : (panel + 1) * LANES]
            if step < 6:
                parcels_a[chip, step] = block
            else:
                parcels_b[chip, step - 6] = block
        for part in range(2):
            parcels_b[chip, 3 + part] = pool[part * 32 : part * 32 + 32, chip * LANES : (chip + 1) * LANES]
    pl.semaphore_wait(barrier, len(partners))

    rows = pl.ds(pl.multiple_of(here * 32, 32), 32)
    parcels, landed = [parcels_a, parcels_b], [landed_a, landed_b]

    def exchange(g):
        copies = []
        for slot, (dx, dy) in enumerate(offsets):
            to_x, to_y = (x + dx) % 4, (y + dy) % 4
            copies.append(
                remote(
                    parcels[g].at[to_x * 4 + to_y],
                    landed[g].at[:, rows, :],
                    plane_send.at[g, slot],
                    plane_recv.at[g, slot],
                    device(to_x, to_y, z, core),
                )
            )
        own = pltpu.make_async_copy(parcels[g].at[here], landed[g].at[:, rows, :], local.at[2 + g])
        own.start()
        own.wait()
        return copies

    half = y % 2

    def block_of(step):
        block = rows_dot(landed_a[half], landed_a[step] if step < 6 else landed_b[step - 6])
        if step < 2:
            down = lax.broadcasted_iota(jnp.int32, block.shape, 0)
            along = lax.broadcasted_iota(jnp.int32, block.shape, 1)
            block = jnp.where((down == along) & (half == step), 0.0, block)
        return block

    def reduce_begin(g):
        remote(partial.at[g, 1 - core], other.at[g], core_send.at[g], core_recv.at[g], twin).wait()
        if g == 0:
            mine[g] = (partial[g, core] + other[g]).astype(BF16)
        else:
            mine[g, :, :640] = (partial[g, core, :, :640] + other[g, :, :640]).astype(BF16)
            squares = partial[g, core, 0:1, 640:] + other[g, 0:1, 640:]
            mine[g, 0:16, 640:] = in_three(squares, 16).astype(BF16)
            mine[g, 16:64, 640:] = jnp.zeros((48, LANES), BF16)
        own = pltpu.make_async_copy(tiles(mine.at[g], z), terms.at[g, 0], local.at[4 + g])
        own.start()
        copies = {
            o: remote(tiles(mine.at[g], column[o]), terms.at[g, o], send.at[g, o], recv.at[g, o], device(x, y, column[o], core))
            for o in far_first
        }
        own.wait()
        return copies

    def tiles(ref, k):
        return ref.at[pl.ds(pl.multiple_of((k // 2) * 8, 8), 8), pl.ds(pl.multiple_of((k % 2) * 384, 384), 384)]

    def slab(g):
        return everything.at[x, y, core, :, pl.ds(g * 768, 768)]

    pending = []

    def reduce_end(g, copies):
        total = terms[g, 0].astype(F32)
        for o in reversed(far_first):
            copies[o].wait()
            total += terms[g, o].astype(F32)
        if g == 0:
            chunk[g] = total.astype(BF16)
        else:
            squares = total[0:1, 256:] + total[1:2, 256:] + total[2:3, 256:]
            chunk[g, :, :256] = total[:, :256].astype(BF16)
            chunk[g, :, 256:] = jnp.where(z == 1, in_three(squares, 8), total[:, 256:]).astype(BF16)
        own = pltpu.make_async_copy(chunk.at[g], tiles(slab(g), z), local.at[6 + g])
        own.start()
        for o in far_first:
            pending.append(
                remote(chunk.at[g], tiles(slab(g), z), send_back.at[g, o], recv_back.at[g, z], device(x, y, column[o], core))
            )
        own.wait()

    def gathered(g, k):
        pltpu.make_async_remote_copy(
            src_ref=chunk.at[g],
            dst_ref=tiles(slab(g), k),
            send_sem=send_back.at[g, 0],
            recv_sem=recv_back.at[g, k],
            device_id=twin,
            device_id_type=MESH,
        ).wait_recv()

    zone = z // 4
    counter = iter(range(200))

    class Strip:
        def __init__(self, group, shift, flip, sign):
            self.group = group
            self.a = (zone + shift) % 4
            self.shift, self.flip, self.sign = shift, flip, sign
            self.place = (pl.ds(pl.multiple_of(self.a * 16, 16), 16), pl.ds(group * 768, 768))
            p, q = (y, x) if flip else (x, y)
            self.p = [p, (p + 4 - sign) % 4, (p + 4 + sign) % 4, (p + 2) % 4]
            self.q = [q, (q + 4 - sign) % 4, (q + 4 + sign) % 4, (q + 2) % 4]
            self.ahead, self.behind = [], []
            self.onward = []

        def where(self, p, q):
            return device(q, p, z, core) if self.flip else device(p, q, z, core)

        def piece(self, p, q):
            return everything.at[(q, p, core) + self.place] if self.flip else everything.at[(p, q, core) + self.place]

        def line(self, q):
            every = slice(None)
            return everything.at[(q, every, core) + self.place] if self.flip else everything.at[(every, q, core) + self.place]

        def go(self, ref, target):
            n = next(counter)
            copy = remote(ref, ref, piece_send.at[n], piece_recv.at[n], target)
            pending.append(copy)
            return copy

        def across(self, n):
            piece = self.piece(self.p[n], self.q[0])
            self.ahead.append(self.go(piece, self.where(self.p[0], self.q[2])))
            self.behind.append(self.go(piece, self.where(self.p[0], self.q[1])))

        def begin(self):
            if self.shift == 0:
                for step in range(1, 4):
                    gathered(self.group, zone * 4 + (z + step) % 4)
            else:
                for step in range(4):
                    gathered(self.group, self.a * 4 + step)
            piece = self.piece(self.p[0], self.q[0])
            self.up = self.go(piece, self.where(self.p[2], self.q[0]))
            self.down = self.go(piece, self.where(self.p[1], self.q[0]))
            self.across(0)

        def second(self):
            self.up.wait_recv()
            self.far = self.go(self.piece(self.p[1], self.q[0]), self.where(self.p[2], self.q[0]))
            self.across(1)
            self.down.wait_recv()
            self.across(2)

        def third(self):
            self.far.wait_recv()
            self.across(3)
            self.twins = [self.go(self.line(self.q[0]), twin)]

        def fourth(self):
            for n in range(4):
                self.ahead[n].wait_recv()
                self.onward.append(self.go(self.piece(self.p[n], self.q[1]), self.where(self.p[0], self.q[2])))
            self.twins.append(self.go(self.line(self.q[1]), twin))
            for n in range(4):
                self.behind[n].wait_recv()
            self.twins.append(self.go(self.line(self.q[2]), twin))

        def fifth(self):
            for copy in self.onward:
                copy.wait_recv()
            self.twins.append(self.go(self.line(self.q[3]), twin))

        def last(self):
            for copy in self.twins:
                copy.wait_recv()

    def strips(g):
        return [Strip(g, 0, False, 1), Strip(g, 1, True, 1), Strip(g, 3, False, -1), Strip(g, 2, True, -1)]

    first = exchange(0)
    row = lax.broadcasted_iota(jnp.int32, (512, 256), 0)
    owner = ((z // 4) * 4 + ((row >> 5) & 3)) * 32 + (row >> 7) * 8 + (z % 4) * 2 + core
    row_id = owner * 64 + (row & 31)
    chosen = [jnp.where(row_id + part * 32 == centers[...], 1.0, 0.0).astype(BF16) for part in range(2)]
    for copy in first:
        copy.wait_send()
    second = exchange(1)
    for copy in first:
        copy.wait_recv()
    for step in range(6):
        block = block_of(step)
        lanes = slice(step * LANES, (step + 1) * LANES)
        partial[0, 0, :, lanes] = block[:64]
        partial[0, 1, :, lanes] = block[64:]
    sums_a = reduce_begin(0)
    wide = landed_a[half].astype(F32)
    squares = jnp.sum(wide * wide, axis=0, keepdims=True)
    top = lax.broadcasted_iota(jnp.int32, (64, LANES), 0) == 0
    for side in range(2):
        partial[1, side, :, 640:] = jnp.where(top, squares, 0.0)
    for copy in second:
        copy.wait()
    for step in range(6, PANELS):
        block = block_of(step)
        lanes = slice((step - 6) * LANES, (step - 5) * LANES)
        partial[1, 0, :, lanes] = block[:64]
        partial[1, 1, :, lanes] = block[64:]
    picked = rows_dot(chosen[0], landed_b[3]) + rows_dot(chosen[1], landed_b[4])
    for part in range(4):
        lanes = slice(384 + (part % 2) * LANES, 384 + (part % 2 + 1) * LANES)
        partial[1, part // 2, :, lanes] = picked[part * 64 : part * 64 + 64]
    sums_b = reduce_begin(1)
    reduce_end(0, sums_a)
    a0, a1, a2, a3 = strips(0)
    b0, b1, b2, b3 = strips(1)
    a0.begin()
    reduce_end(1, sums_b)
    a0.second(), a1.begin(), a2.begin(), a3.begin(), a0.third()
    a1.second(), a2.second(), b0.begin(), a3.second(), a1.third(), a2.third(), a3.third()
    b1.begin(), b2.begin(), a0.fourth(), b0.second(), b3.begin(), a1.fourth(), a2.fourth()
    b1.second(), b2.second(), b0.third(), a3.fourth(), b3.second(), a0.fifth(), b1.third(), b2.third(), b3.third()
    a1.fifth(), a2.fifth(), a3.fifth(), b0.fourth(), b1.fourth(), b2.fourth(), b3.fourth()
    b0.fifth(), b1.fifth(), b2.fifth(), b3.fifth()
    for strip in (a0, a1, a2, a3, b0, b1, b2, b3):
        strip.last()
    for copy in pending:
        copy.wait_send()


def whiten_kernel(sample_total, blocks, pool, whitened, start, held, ready, corner, scale, extra):
    count = start.shape[0]
    for chip in range(16):
        lanes = slice(chip * LANES, (chip + 1) * LANES)
        parts = blocks[chip * LANES : chip * LANES + 16, DIAG:].astype(F32)
        mean = (parts[0:1] + parts[1:2] + parts[2:3]) / sample_total
        inverse = 1.0 / jnp.sqrt(mean + EPSILON)
        scale[0:1, lanes] = inverse
        extra[0:1, lanes] = inverse * mean * inverse - 1.0
        for part in range(4):
            rows = slice(chip * LANES + (part // 2) * 64, chip * LANES + (part // 2) * 64 + 64)
            source = slice(GRAM + (part % 2) * LANES, GRAM + (part % 2 + 1) * LANES)
            start[part * 64 : part * 64 + 64, lanes] = blocks[rows, source].astype(F32) * inverse
        start[256:, lanes] = pool[:, lanes].astype(F32) * inverse
    for pair in range(4):
        for half in range(2):
            rows = slice(half * LANES, (half + 1) * LANES)
            others = slice((1 - half) * LANES, (2 - half) * LANES)
            top = (2 * pair + half) * LANES
            corner[pair, rows, rows] = blocks[top : top + LANES, GRAM - LANES : GRAM]
            top = (2 * pair + 8 + half) * LANES
            corner[pair, others, rows] = blocks[top : top + LANES, GRAM - LANES : GRAM].astype(F32).T.astype(BF16)
    held[...] = start[...] * (1.0 / 16.0)

    def transposed(left, right):
        return lax.dot_general(left, right, (((1,), (1,)), ((), ())), preferred_element_type=F32)

    @pl.loop(0, 4)
    def _(turn):
        factor = jnp.where(turn == 0, -0.3125, jnp.where(turn == 1, 0.375, jnp.where(turn == 2, -0.5, 1.0)))
        for j in range(8):
            lanes = slice(j * 256, (j + 1) * 256)
            scaled = (held[:, lanes] * scale[0:1, lanes]).astype(BF16)
            ready[:, lanes] = scaled
            if j < 3:
                ready[:, 2048 + j * 256 : 2048 + (j + 1) * 256] = scaled
        for j in range(8):
            lanes = slice(j * 256, (j + 1) * 256)
            out = transposed(ready[:, (j + 1) * 256 : (j + 4) * 256], blocks[lanes, 256:1024])
            for d in range(4):
                i = (j - d) % 8
                out += jnp.dot(
                    ready[:, i * 256 : (i + 1) * 256],
                    blocks[i * 256 : (i + 1) * 256, d * 256 : (d + 1) * 256],
                    preferred_element_type=F32,
                )
            if j >= 4:
                out += jnp.dot(ready[:, (j - 4) * 256 : (j - 3) * 256], corner[j - 4], preferred_element_type=F32)
            else:
                out += transposed(ready[:, (j + 4) * 256 : (j + 5) * 256], corner[j])
            held[:, lanes] = (
                out * (scale[0:1, lanes] * (1.0 / sample_total))
                + held[:, lanes] * extra[0:1, lanes]
                + factor * start[:, lanes]
            )

    whitened[...] = held[...].astype(BF16)


VMEM = pl.BlockSpec(memory_space=pltpu.VMEM)
HBM = pl.BlockSpec(memory_space=pltpu.HBM)
DMA = pltpu.SemaphoreType.DMA


def parameters(collective=None, limit=48):
    if collective is None:
        return pltpu.CompilerParams(vmem_limit_bytes=limit * 1024 * 1024)
    return pltpu.CompilerParams(collective_id=collective, has_side_effects=True, vmem_limit_bytes=limit * 1024 * 1024)


def squared_terms(row_values, centre_rows):
    row_wide = row_values.astype(F32)
    centre_wide = centre_rows.astype(F32)
    row_norms = jnp.sum(row_wide * row_wide, axis=1)
    centre_norms = jnp.sum(centre_wide * centre_wide, axis=1)
    inner_products = lax.dot_general(row_values, centre_rows, (((1,), (1,)), ((), ())), preferred_element_type=F32)
    return row_norms[:, None] + centre_norms[None, :] - 2.0 * inner_products


def per_device(sample, pool, old_min, centers):
    width = sample.shape[1]
    pool_count = pool.shape[0]
    sample_total = sample.shape[0] * lax.axis_size("dp") * lax.axis_size("feat")
    everything = pl.pallas_call(
        moments_kernel,
        out_shape=jax.ShapeDtypeStruct((4, 4, 2, 64, SLAB), BF16),
        in_specs=[HBM, HBM, VMEM],
        out_specs=VMEM,
        scratch_shapes=[
            pltpu.VMEM(sample.shape, BF16),
            pltpu.VMEM(pool.shape, BF16),
            pltpu.VMEM((16, 6, 32, LANES), BF16),
            pltpu.VMEM((16, 5, 32, LANES), BF16),
            pltpu.VMEM((6, 512, LANES), BF16),
            pltpu.VMEM((5, 512, LANES), BF16),
            pltpu.VMEM((2, 2, 64, 768), F32),
            pltpu.VMEM((2, 64, 768), F32),
            pltpu.VMEM((2, 64, 768), BF16),
            pltpu.VMEM((2, 16, 8, 384), BF16),
            pltpu.VMEM((2, 8, 384), BF16),
            DMA((8,)),
            DMA((2, 15)),
            DMA((2, 15)),
            DMA((2,)),
            DMA((2,)),
            DMA((2, 16)),
            DMA((2, 16)),
            DMA((2, 16)),
            DMA((2, 16)),
            DMA((152,)),
            DMA((152,)),
        ],
        compiler_params=parameters(0, 16),
    )(sample, pool, centers.reshape(1, 256))
    count = 256 + pool_count
    whitened = pl.pallas_call(
        lambda *refs: whiten_kernel(float(sample_total), *refs),
        out_shape=jax.ShapeDtypeStruct((count, width), BF16),
        in_specs=[VMEM, VMEM],
        out_specs=VMEM,
        scratch_shapes=[
            pltpu.VMEM((count, width), F32),
            pltpu.VMEM((count, width), F32),
            pltpu.VMEM((count, width + 768), BF16),
            pltpu.VMEM((4, 256, 256), BF16),
            pltpu.VMEM((8, width), F32),
            pltpu.VMEM((8, width), F32),
        ],
        compiler_params=parameters(None, 24),
    )(everything.reshape(width, SLAB), pool)
    squared = squared_terms(whitened[256:], whitened[:256])
    nearest = jnp.min(jnp.maximum(squared, 0.0), axis=1) / (2.0 * width)
    return jnp.minimum(old_min, nearest)


def solution(mesh):
    return jax.shard_map(
        per_device,
        mesh=mesh,
        in_specs=(P(("dp", "feat"), None), P(("dp", "feat"), None), P(("dp", "feat")), P()),
        out_specs=P(("dp", "feat")),
        check_vma=False,
    )
```

```python
import jax
import jax.numpy as jnp
from jax import lax
from jax.experimental import pallas as pl
from jax.experimental.pallas import tpu as pltpu
from jax.sharding import PartitionSpec as P

EPSILON = 1e-06
MESH = pl.DeviceIdType.MESH
F32 = jnp.float32
BF16 = jnp.bfloat16
LANES = 128
PANELS = 9
SLAB = 1536
GRAM = PANELS * LANES
DIAG = SLAB - LANES


def position():
    dp = lax.axis_index("dp")
    feat = lax.axis_index("feat")
    x, y = feat // 8, dp % 4
    z = (dp // 4) * 4 + (feat // 2) % 4
    return x, y, z, feat % 2


def device(x, y, z, core):
    return ((z // 4) * 4 + y, x * 8 + (z % 4) * 2 + core)


def remote(src, dst, send, recv, where):
    copy = pltpu.make_async_remote_copy(
        src_ref=src, dst_ref=dst, send_sem=send, recv_sem=recv, device_id=where, device_id_type=MESH
    )
    copy.start()
    return copy


def column_panels(chip):
    pair, half = chip // 2, chip % 2
    last = half if pair < 4 else 1 - half
    return [(2 * pair + step) % 16 for step in range(8)] + [(2 * pair + 8 + last) % 16]


def in_three(total, count):
    high = total.astype(BF16).astype(F32)
    middle = (total - high).astype(BF16).astype(F32)
    low = total - high - middle
    rows = lax.broadcasted_iota(jnp.int32, (count, LANES), 0)
    return jnp.where(rows == 0, high, jnp.where(rows == 1, middle, jnp.where(rows == 2, low, 0.0)))


def rows_dot(left, right):
    return lax.dot_general(left, right, (((0,), (0,)), ((), ())), preferred_element_type=F32)


def lanes_dot(left, right):
    return lax.dot_general(left, right, (((1,), (1,)), ((), ())), preferred_element_type=F32)


def update_kernel(
    sample_total, sample_in, pool_in, centers, nearest, sample, pool, parcels_a, parcels_b, landed_a, landed_b, partial, other, mine,
    terms, chunk, everything, start, held, ready, corner, scale, extra, whitened, twin_rows, local, plane_send, plane_recv,
    core_send, core_recv, send, recv, send_back, recv_back, strip_send, strip_recv,
):
    x, y, z, core = position()
    here = x * 4 + y
    twin = device(x, y, z, 1 - core)
    column = [(z + o) % 16 for o in range(16)]
    far_first = [8] + [o for d in range(7, 0, -1) for o in (d, 16 - d)]
    offsets = [(dx, dy) for dx in range(4) for dy in range(4) if dx or dy]
    loads = [
        pltpu.make_async_copy(sample_in, sample, local.at[0]),
        pltpu.make_async_copy(pool_in, pool, local.at[1]),
    ]
    for copy in loads:
        copy.start()
    barrier = pltpu.get_barrier_semaphore()
    partners = [device(x, y, column[o], core) for o in far_first]
    partners += [device((x + dx) % 4, (y + dy) % 4, z, core) for dx, dy in offsets] + [twin]
    for partner in partners:
        pl.semaphore_signal(barrier, inc=1, device_id=partner, device_id_type=MESH)

    for copy in loads:
        copy.wait()
    for chip in range(16):
        for step, panel in enumerate(column_panels(chip)):
            block = sample[:, panel * LANES : (panel + 1) * LANES]
            if step < 6:
                parcels_a[chip, step] = block
            else:
                parcels_b[chip, step - 6] = block
        for part in range(2):
            parcels_b[chip, 3 + part] = pool[part * 32 : part * 32 + 32, chip * LANES : (chip + 1) * LANES]
    pl.semaphore_wait(barrier, len(partners))

    def bytes_of(ref, send_sem, recv_sem):
        return pltpu.make_async_remote_copy(
            src_ref=ref, dst_ref=ref, send_sem=send_sem, recv_sem=recv_sem, device_id=twin, device_id_type=MESH
        )

    rows = pl.ds(pl.multiple_of(here * 32, 32), 32)
    parcels, landed = [parcels_a, parcels_b], [landed_a, landed_b]

    def exchange(g):
        for dx, dy in offsets:
            to_x, to_y = (x + dx) % 4, (y + dy) % 4
            remote(
                parcels[g].at[to_x * 4 + to_y],
                landed[g].at[:, rows, :],
                plane_send.at[g],
                plane_recv.at[g],
                device(to_x, to_y, z, core),
            )
        own = pltpu.make_async_copy(parcels[g].at[here], landed[g].at[:, rows, :], local.at[2 + g])
        own.start()
        own.wait()
        return bytes_of(landed[g].at[:, pl.ds(0, 480), :], plane_send.at[g], plane_recv.at[g])

    half = y % 2

    def block_of(step):
        block = rows_dot(landed_a[half], landed_a[step] if step < 6 else landed_b[step - 6])
        if step < 2:
            down = lax.broadcasted_iota(jnp.int32, block.shape, 0)
            along = lax.broadcasted_iota(jnp.int32, block.shape, 1)
            block = jnp.where((down == along) & (half == step), 0.0, block)
        return block

    def tiles(ref, k):
        return ref.at[pl.ds(pl.multiple_of((k // 2) * 8, 8), 8), pl.ds(pl.multiple_of((k % 2) * 384, 384), 384)]

    def slab(g):
        return everything.at[x, y, core, :, pl.ds(g * 768, 768)]

    def reduce_begin(g):
        remote(partial.at[g, 1 - core], other.at[g], core_send.at[g], core_recv.at[g], twin).wait()
        if g == 0:
            mine[g] = (partial[g, core] + other[g]).astype(BF16)
        else:
            mine[g, :, :640] = (partial[g, core, :, :640] + other[g, :, :640]).astype(BF16)
            squares = partial[g, core, 0:1, 640:] + other[g, 0:1, 640:]
            mine[g, 0:16, 640:] = in_three(squares, 16).astype(BF16)
            mine[g, 16:64, 640:] = jnp.zeros((48, LANES), BF16)
        own = pltpu.make_async_copy(tiles(mine.at[g], z), terms.at[g, 0], local.at[4 + g])
        own.start()
        for o in far_first:
            remote(tiles(mine.at[g], column[o]), terms.at[g, o], send.at[g], recv.at[g], device(x, y, column[o], core))
        own.wait()

    def reduce_end(g):
        bytes_of(terms.at[g, pl.ds(1, 15)], send.at[g], recv.at[g]).wait()
        total = terms[g, 0].astype(F32)
        for o in range(1, 16):
            total += terms[g, o].astype(F32)
        if g == 0:
            chunk[g] = total.astype(BF16)
        else:
            squares = total[0:1, 256:] + total[1:2, 256:] + total[2:3, 256:]
            chunk[g, :, :256] = total[:, :256].astype(BF16)
            chunk[g, :, 256:] = jnp.where(z == 1, in_three(squares, 8), total[:, 256:]).astype(BF16)
        own = pltpu.make_async_copy(chunk.at[g], tiles(slab(g), z), local.at[6 + g])
        own.start()
        for o in far_first:
            remote(chunk.at[g], tiles(slab(g), z), send_back.at[g], recv_back.at[g, z // 4], device(x, y, column[o], core))
        own.wait()

    zone = z // 4

    class Strip:
        def __init__(self, group, shift, flip):
            self.group, self.shift, self.flip = group, shift, flip
            self.a = (zone + shift) % 4
            self.place = (pl.ds(pl.multiple_of(self.a * 16, 16), 16), pl.ds(group * 768, 768))
            p, q = (y, x) if flip else (x, y)
            self.p = [(p + 4 - d) % 4 for d in range(4)]
            self.q = [(q + 4 - d) % 4 for d in range(4)]
            number = group * 4 + shift
            self.sent = [strip_send.at[number, n] for n in range(2)]
            self.got = [strip_recv.at[number, n] for n in range(7)]

        def where(self, p, q):
            return device(q, p, z, core) if self.flip else device(p, q, z, core)

        def piece(self, p, q):
            return everything.at[(q, p, core) + self.place] if self.flip else everything.at[(p, q, core) + self.place]

        def line(self, q, side=None):
            every, side = slice(None), core if side is None else side
            return everything.at[(q, every, side) + self.place] if self.flip else everything.at[(every, q, side) + self.place]

        def across(self, n):
            piece = self.piece(self.p[n], self.q[0])
            for d in (2, 1, 3):
                remote(piece, piece, self.sent[0], self.got[3 + d - 1], self.where(self.p[0], self.q[4 - d]))

        def twins(self, d):
            line = self.line(self.q[d])
            remote(line, line, self.sent[1], self.got[6], twin)

        def begin(self):
            if self.shift == 0:
                ref = terms.at[self.group, pl.ds(0, 3)]
            else:
                ref = self.piece(self.p[0], self.q[0])
            bytes_of(ref, send_back.at[self.group], recv_back.at[self.group, self.a]).wait_recv()
            piece = self.piece(self.p[0], self.q[0])
            for d in (2, 1, 3):
                remote(piece, piece, self.sent[0], self.got[d - 1], self.where(self.p[4 - d], self.q[0]))
            self.across(0)

        def middle(self):
            for d in (1, 3, 2):
                bytes_of(self.piece(self.p[d], self.q[0]), self.sent[0], self.got[d - 1]).wait_recv()
                self.across(d)
            self.twins(0)

        def finish(self):
            for d in (1, 3, 2):
                bytes_of(self.line(self.q[d]), self.sent[0], self.got[3 + d - 1]).wait_recv()
                self.twins(d)

        def last(self):
            whole = everything.at[(slice(None), slice(None), 1 - core) + self.place]
            bytes_of(whole, self.sent[1], self.got[6]).wait()
            bytes_of(landed_a.at[pl.ds(0, 3), pl.ds(0, 480), :], self.sent[0], self.got[0]).wait_send()

    first = exchange(0)
    row = lax.broadcasted_iota(jnp.int32, (512, 256), 0)
    owner = ((z // 4) * 4 + ((row >> 5) & 3)) * 32 + (row >> 7) * 8 + (z % 4) * 2 + core
    row_id = owner * 64 + (row & 31)
    chosen = [jnp.where(row_id + part * 32 == centers[...], 1.0, 0.0).astype(BF16) for part in range(2)]
    first.wait_send()
    second = exchange(1)
    first.wait_recv()
    for step in range(6):
        block = block_of(step)
        lanes = slice(step * LANES, (step + 1) * LANES)
        partial[0, 0, :, lanes] = block[:64]
        partial[0, 1, :, lanes] = block[64:]
    reduce_begin(0)
    wide = landed_a[half].astype(F32)
    squares = jnp.sum(wide * wide, axis=0, keepdims=True)
    top = lax.broadcasted_iota(jnp.int32, (64, LANES), 0) == 0
    for side in range(2):
        partial[1, side, :, 640:] = jnp.where(top, squares, 0.0)
    second.wait()
    for step in range(6, PANELS):
        block = block_of(step)
        lanes = slice((step - 6) * LANES, (step - 5) * LANES)
        partial[1, 0, :, lanes] = block[:64]
        partial[1, 1, :, lanes] = block[64:]
    picked = rows_dot(chosen[0], landed_b[3]) + rows_dot(chosen[1], landed_b[4])
    for part in range(4):
        lanes = slice(384 + (part % 2) * LANES, 384 + (part % 2 + 1) * LANES)
        partial[1, part // 2, :, lanes] = picked[part * 64 : part * 64 + 64]
    reduce_begin(1)
    reduce_end(0)
    a0, a1, a2, a3 = [Strip(0, shift, shift % 2 == 1) for shift in (0, 1, 3, 2)]
    b0, b1, b2, b3 = [Strip(1, shift, shift % 2 == 1) for shift in (0, 1, 3, 2)]
    a0.begin()
    a0.middle()
    reduce_end(1)
    a1.begin(), a2.begin(), a3.begin()
    a1.middle(), a2.middle(), b0.begin(), a3.middle(), a0.finish(), b0.middle()
    b1.begin(), b2.begin(), a1.finish(), a2.finish(), b3.begin(), b1.middle(), b2.middle(), b3.middle()
    a3.finish(), b0.finish(), b1.finish(), b2.finish(), b3.finish()
    for strip in (a0, a1, a2, a3, b0, b1, b2, b3):
        strip.last()
    for g in range(2):
        bytes_of(terms.at[g, pl.ds(1, 15)], send_back.at[g], recv_back.at[g, 0]).wait_send()

    def blocks(i, low, high):
        return everything[i // 2, 2 * (i % 2) : 2 * (i % 2) + 2, :, :, low:high].reshape(256, high - low)

    for chip in range(16):
        lanes = slice(chip * LANES, (chip + 1) * LANES)
        parts = everything[chip // 4, chip % 4, 0, 0:16, DIAG:].astype(F32)
        mean = (parts[0:1] + parts[1:2] + parts[2:3]) / sample_total
        inverse = 1.0 / jnp.sqrt(mean + EPSILON)
        scale[0:1, lanes] = inverse
        extra[0:1, lanes] = inverse * mean * inverse - 1.0
        for part in range(2):
            source = slice(GRAM + part * LANES, GRAM + (part + 1) * LANES)
            start[part * 64 : part * 64 + 64, lanes] = everything[chip // 4, chip % 4, core, :, source].astype(F32) * inverse
        start[128:, lanes] = pool[:, lanes].astype(F32) * inverse
    for pair in range(4):
        for side in range(2):
            span = slice(side * LANES, (side + 1) * LANES)
            others = slice((1 - side) * LANES, (2 - side) * LANES)
            corner[pair, span, span] = blocks(pair, GRAM - LANES, GRAM)[span]
            corner[pair, others, span] = blocks(pair + 4, GRAM - LANES, GRAM)[span].astype(F32).T.astype(BF16)
    held[...] = start[...] * (1.0 / 16.0)

    @pl.loop(0, 4)
    def _(turn):
        factor = jnp.where(turn == 0, -0.3125, jnp.where(turn == 1, 0.375, jnp.where(turn == 2, -0.5, 1.0)))
        for j in range(8):
            lanes = slice(j * 256, (j + 1) * 256)
            scaled = (held[:, lanes] * scale[0:1, lanes]).astype(BF16)
            ready[:, lanes] = scaled
            if j < 3:
                ready[:, 2048 + j * 256 : 2048 + (j + 1) * 256] = scaled
        for j in range(8):
            lanes = slice(j * 256, (j + 1) * 256)
            out = lanes_dot(ready[:, (j + 1) * 256 : (j + 4) * 256], blocks(j, 256, 1024))
            for d in range(4):
                i = (j - d) % 8
                out += jnp.dot(
                    ready[:, i * 256 : (i + 1) * 256], blocks(i, d * 256, (d + 1) * 256), preferred_element_type=F32
                )
            if j >= 4:
                out += jnp.dot(ready[:, (j - 4) * 256 : (j - 3) * 256], corner[j - 4], preferred_element_type=F32)
            else:
                out += lanes_dot(ready[:, (j + 4) * 256 : (j + 5) * 256], corner[j])
            held[:, lanes] = (
                out * (scale[0:1, lanes] * (1.0 / sample_total))
                + held[:, lanes] * extra[0:1, lanes]
                + factor * start[:, lanes]
            )

    whitened[...] = held[...].astype(BF16)
    swap = remote(whitened.at[pl.ds(0, 128)], twin_rows, core_send.at[2], core_recv.at[2], twin)
    wide = whitened[128:].astype(F32)
    squares = wide * wide
    ones = jnp.ones((8, LANES), BF16)
    row_norms = jnp.zeros((8, 64), F32)
    for chip in range(16):
        part = squares[:, chip * LANES : (chip + 1) * LANES]
        for _ in range(3):
            piece = part.astype(BF16)
            row_norms += lanes_dot(ones, piece)
            part -= piece.astype(F32)

    def closest(centre_rows):
        wide = centre_rows.astype(F32)
        norms = jnp.sum(wide * wide, axis=1, keepdims=True)
        squared = row_norms[0:1] + norms - 2.0 * lanes_dot(centre_rows, whitened[128:])
        return jnp.min(jnp.maximum(squared, 0.0), axis=0, keepdims=True)

    best = closest(whitened[0:128])
    swap.wait()
    best = jnp.minimum(best, closest(twin_rows[...]))
    nearest[...] = best / (2.0 * 16 * LANES)


VMEM = pl.BlockSpec(memory_space=pltpu.VMEM)
HBM = pl.BlockSpec(memory_space=pltpu.HBM)
DMA = pltpu.SemaphoreType.DMA
LIMIT = 56 * 1024 * 1024


def per_device(sample, pool, old_min, centers):
    width = sample.shape[1]
    sample_total = sample.shape[0] * lax.axis_size("dp") * lax.axis_size("feat")
    nearest = pl.pallas_call(
        lambda *refs: update_kernel(float(sample_total), *refs),
        out_shape=jax.ShapeDtypeStruct((1, pool.shape[0]), F32),
        in_specs=[HBM, HBM, VMEM],
        out_specs=VMEM,
        scratch_shapes=[
            pltpu.VMEM(sample.shape, BF16),
            pltpu.VMEM(pool.shape, BF16),
            pltpu.VMEM((16, 6, 32, LANES), BF16),
            pltpu.VMEM((16, 5, 32, LANES), BF16),
            pltpu.VMEM((6, 512, LANES), BF16),
            pltpu.VMEM((5, 512, LANES), BF16),
            pltpu.VMEM((2, 2, 64, 768), F32),
            pltpu.VMEM((2, 64, 768), F32),
            pltpu.VMEM((2, 64, 768), BF16),
            pltpu.VMEM((2, 16, 8, 384), BF16),
            pltpu.VMEM((2, 8, 384), BF16),
            pltpu.VMEM((4, 4, 2, 64, SLAB), BF16),
            pltpu.VMEM((192, width), F32),
            pltpu.VMEM((192, width), F32),
            pltpu.VMEM((192, width + 768), BF16),
            pltpu.VMEM((4, 256, 256), BF16),
            pltpu.VMEM((8, width), F32),
            pltpu.VMEM((8, width), F32),
            pltpu.VMEM((192, width), BF16),
            pltpu.VMEM((128, width), BF16),
            DMA((8,)),
            DMA((2,)),
            DMA((2,)),
            DMA((3,)),
            DMA((3,)),
            DMA((2,)),
            DMA((2,)),
            DMA((2,)),
            DMA((2, 4)),
            DMA((8, 2)),
            DMA((8, 7)),
        ],
        compiler_params=pltpu.CompilerParams(collective_id=0, has_side_effects=True, vmem_limit_bytes=LIMIT),
    )(sample, pool, centers.reshape(1, 256))
    return jnp.minimum(old_min, nearest.reshape(old_min.shape))


def solution(mesh):
    return jax.shard_map(
        per_device,
        mesh=mesh,
        in_specs=(P(("dp", "feat"), None), P(("dp", "feat"), None), P(("dp", "feat")), P()),
        out_specs=P(("dp", "feat")),
        check_vma=False,
    )
```

```python
import jax
import jax.numpy as jnp
from jax import lax
from jax.experimental import pallas as pl
from jax.experimental.pallas import tpu as pltpu
from jax.sharding import PartitionSpec as P

EPSILON = 1e-06
MESH = pl.DeviceIdType.MESH
F32 = jnp.float32
BF16 = jnp.bfloat16
LANES = 128
PANELS = 9
SLAB = 1536
GRAM = PANELS * LANES
DIAG = SLAB - LANES


def position():
    dp = lax.axis_index("dp")
    feat = lax.axis_index("feat")
    x, y = feat // 8, dp % 4
    z = (dp // 4) * 4 + (feat // 2) % 4
    return x, y, z, feat % 2


def device(x, y, z, core):
    return ((z // 4) * 4 + y, x * 8 + (z % 4) * 2 + core)


def remote(src, dst, send, recv, where):
    copy = pltpu.make_async_remote_copy(
        src_ref=src, dst_ref=dst, send_sem=send, recv_sem=recv, device_id=where, device_id_type=MESH
    )
    copy.start()
    return copy


def column_panels(chip):
    pair, half = chip // 2, chip % 2
    last = half if pair < 4 else 1 - half
    return [(2 * pair + step) % 16 for step in range(8)] + [(2 * pair + 8 + last) % 16]


def in_three(total, count):
    high = total.astype(BF16).astype(F32)
    middle = (total - high).astype(BF16).astype(F32)
    low = total - high - middle
    rows = lax.broadcasted_iota(jnp.int32, (count, LANES), 0)
    return jnp.where(rows == 0, high, jnp.where(rows == 1, middle, jnp.where(rows == 2, low, 0.0)))


def rows_dot(left, right):
    return lax.dot_general(left, right, (((0,), (0,)), ((), ())), preferred_element_type=F32)


def lanes_dot(left, right):
    return lax.dot_general(left, right, (((1,), (1,)), ((), ())), preferred_element_type=F32)


def update_kernel(
    sample_total, sample_in, pool_in, centers, nearest, sample, pool, parcels_a, parcels_b, landed_a, landed_b, partial, other, mine,
    terms, chunk, everything, start, held, ready, corner, scale, extra, whitened, twin_rows, local, plane_send, plane_recv,
    core_send, core_recv, send, recv, send_back, recv_back, strip_send, strip_recv,
):
    x, y, z, core = position()
    here = x * 4 + y
    twin = device(x, y, z, 1 - core)
    column = [(z + o) % 16 for o in range(16)]
    far_first = [8] + [o for d in range(7, 0, -1) for o in (d, 16 - d)]
    offsets = [(dx, dy) for dx in range(4) for dy in range(4) if dx or dy]
    loads = [
        pltpu.make_async_copy(sample_in, sample, local.at[0]),
        pltpu.make_async_copy(pool_in, pool, local.at[1]),
    ]
    for copy in loads:
        copy.start()
    barrier = pltpu.get_barrier_semaphore()
    partners = [device(x, y, column[o], core) for o in far_first]
    partners += [device((x + dx) % 4, (y + dy) % 4, z, core) for dx, dy in offsets] + [twin]
    for partner in partners:
        pl.semaphore_signal(barrier, inc=1, device_id=partner, device_id_type=MESH)

    for copy in loads:
        copy.wait()
    for chip in range(16):
        for step, panel in enumerate(column_panels(chip)):
            block = sample[:, panel * LANES : (panel + 1) * LANES]
            if step < 6:
                parcels_a[chip, step] = block
            else:
                parcels_b[chip, step - 6] = block
        for part in range(2):
            parcels_b[chip, 3 + part] = pool[part * 32 : part * 32 + 32, chip * LANES : (chip + 1) * LANES]
    pl.semaphore_wait(barrier, len(partners))

    def bytes_of(ref, send_sem, recv_sem):
        return pltpu.make_async_remote_copy(
            src_ref=ref, dst_ref=ref, send_sem=send_sem, recv_sem=recv_sem, device_id=twin, device_id_type=MESH
        )

    rows = pl.ds(pl.multiple_of(here * 32, 32), 32)
    parcels, landed = [parcels_a, parcels_b], [landed_a, landed_b]

    def exchange(g):
        for dx, dy in offsets:
            to_x, to_y = (x + dx) % 4, (y + dy) % 4
            remote(
                parcels[g].at[to_x * 4 + to_y],
                landed[g].at[:, rows, :],
                plane_send.at[g],
                plane_recv.at[g],
                device(to_x, to_y, z, core),
            )
        own = pltpu.make_async_copy(parcels[g].at[here], landed[g].at[:, rows, :], local.at[2 + g])
        own.start()
        own.wait()
        return bytes_of(landed[g].at[:, pl.ds(0, 480), :], plane_send.at[g], plane_recv.at[g])

    half = y % 2

    def block_of(step):
        block = rows_dot(landed_a[half], landed_a[step] if step < 6 else landed_b[step - 6])
        if step < 2:
            down = lax.broadcasted_iota(jnp.int32, block.shape, 0)
            along = lax.broadcasted_iota(jnp.int32, block.shape, 1)
            block = jnp.where((down == along) & (half == step), 0.0, block)
        return block

    def tiles(ref, k):
        return ref.at[pl.ds(pl.multiple_of((k // 2) * 8, 8), 8), pl.ds(pl.multiple_of((k % 2) * 384, 384), 384)]

    def slab(g):
        return everything.at[x // 2, x % 2, y // 2, y % 2, core, :, pl.ds(g * 768, 768)]

    def reduce_begin(g):
        remote(partial.at[g, 1 - core], other.at[g], core_send.at[g], core_recv.at[g], twin).wait()
        if g == 0:
            mine[g] = (partial[g, core] + other[g]).astype(BF16)
        else:
            mine[g, :, :640] = (partial[g, core, :, :640] + other[g, :, :640]).astype(BF16)
            squares = partial[g, core, 0:1, 640:] + other[g, 0:1, 640:]
            mine[g, 0:16, 640:] = in_three(squares, 16).astype(BF16)
            mine[g, 16:64, 640:] = jnp.zeros((48, LANES), BF16)
        own = pltpu.make_async_copy(tiles(mine.at[g], z), terms.at[g, 0], local.at[4 + g])
        own.start()
        for o in far_first:
            remote(tiles(mine.at[g], column[o]), terms.at[g, o], send.at[g], recv.at[g], device(x, y, column[o], core))
        own.wait()

    def reduce_end(g):
        bytes_of(terms.at[g, pl.ds(1, 15)], send.at[g], recv.at[g]).wait()
        total = terms[g, 0].astype(F32)
        for o in range(1, 16):
            total += terms[g, o].astype(F32)
        if g == 0:
            chunk[g] = total.astype(BF16)
        else:
            squares = total[0:1, 256:] + total[1:2, 256:] + total[2:3, 256:]
            chunk[g, :, :256] = total[:, :256].astype(BF16)
            chunk[g, :, 256:] = jnp.where(z == 1, in_three(squares, 8), total[:, 256:]).astype(BF16)
        own = pltpu.make_async_copy(chunk.at[g], tiles(slab(g), z), local.at[6 + g])
        own.start()
        for o in far_first:
            remote(chunk.at[g], tiles(slab(g), z), send_back.at[g], recv_back.at[g, z // 4], device(x, y, column[o], core))
        own.wait()

    zone = z // 4

    class Strip:
        def __init__(self, group, shift, flip):
            self.group, self.shift, self.flip = group, shift, flip
            self.a = (zone + shift) % 4
            self.place = (pl.ds(pl.multiple_of(self.a * 16, 16), 16), pl.ds(group * 768, 768))
            p, q = (y, x) if flip else (x, y)
            self.p = [(p + 4 - d) % 4 for d in range(4)]
            self.q = [(q + 4 - d) % 4 for d in range(4)]
            number = group * 4 + shift
            self.sent = [strip_send.at[number, n] for n in range(2)]
            self.got = [strip_recv.at[number, n] for n in range(9)]

        def where(self, p, q):
            return device(q, p, z, core) if self.flip else device(p, q, z, core)

        def at(self, p, q):
            first, second = (q, p) if self.flip else (p, q)
            return everything.at[first + second + (core,) + self.place]

        def piece(self, p, q):
            return self.at((p // 2, p % 2), (q // 2, q % 2))

        def pair(self, parity, q):
            return self.at((slice(None), parity), (q // 2, q % 2))

        def line(self, q):
            return self.at((slice(None), slice(None)), (q // 2, q % 2))

        def across(self, n):
            piece = self.piece(self.p[n], self.q[0])
            remote(piece, piece, self.sent[0], self.got[3 + n % 2], self.where(self.p[0], self.q[3]))
            remote(piece, piece, self.sent[0], self.got[5 + n % 2], self.where(self.p[0], self.q[1]))

        def twins(self, d):
            line = self.line(self.q[d])
            remote(line, line, self.sent[1], self.got[8], twin)

        def begin(self):
            if self.shift == 0:
                ref = terms.at[self.group, pl.ds(0, 3)]
            else:
                ref = self.piece(self.p[0], self.q[0])
            bytes_of(ref, send_back.at[self.group], recv_back.at[self.group, self.a]).wait_recv()
            piece = self.piece(self.p[0], self.q[0])
            for d in (2, 1, 3):
                remote(piece, piece, self.sent[0], self.got[d - 1], self.where(self.p[4 - d], self.q[0]))
            self.across(0)

        def middle(self):
            for d in (1, 3, 2):
                bytes_of(self.piece(self.p[d], self.q[0]), self.sent[0], self.got[d - 1]).wait_recv()
                self.across(d)
            self.twins(0)

        def forward(self):
            same, other = self.p[0] % 2, 1 - self.p[0] % 2
            up, down = self.pair(same, self.q[1]), self.pair(other, self.q[3])
            bytes_of(up, self.sent[0], self.got[3]).wait_recv()
            remote(up, up, self.sent[0], self.got[7], self.where(self.p[0], self.q[3]))
            bytes_of(down, self.sent[0], self.got[6]).wait_recv()
            remote(down, down, self.sent[0], self.got[7], self.where(self.p[0], self.q[1]))
            bytes_of(self.pair(other, self.q[1]), self.sent[0], self.got[4]).wait_recv()
            self.twins(1)
            bytes_of(self.pair(same, self.q[3]), self.sent[0], self.got[5]).wait_recv()
            self.twins(3)

        def finish(self):
            bytes_of(self.line(self.q[2]), self.sent[0], self.got[7]).wait_recv()
            self.twins(2)

        def last(self):
            every = slice(None)
            whole = everything.at[(every, every, every, every, 1 - core) + self.place]
            bytes_of(whole, self.sent[1], self.got[8]).wait()
            bytes_of(landed_a.at[pl.ds(0, 3), pl.ds(0, 480), :], self.sent[0], self.got[0]).wait_send()

    first = exchange(0)
    row = lax.broadcasted_iota(jnp.int32, (512, 256), 0)
    owner = ((z // 4) * 4 + ((row >> 5) & 3)) * 32 + (row >> 7) * 8 + (z % 4) * 2 + core
    row_id = owner * 64 + (row & 31)
    chosen = [jnp.where(row_id + part * 32 == centers[...], 1.0, 0.0).astype(BF16) for part in range(2)]
    first.wait_send()
    second = exchange(1)
    first.wait_recv()
    for step in range(6):
        block = block_of(step)
        lanes = slice(step * LANES, (step + 1) * LANES)
        partial[0, 0, :, lanes] = block[:64]
        partial[0, 1, :, lanes] = block[64:]
    reduce_begin(0)
    wide = landed_a[half].astype(F32)
    squares = jnp.sum(wide * wide, axis=0, keepdims=True)
    top = lax.broadcasted_iota(jnp.int32, (64, LANES), 0) == 0
    for side in range(2):
        partial[1, side, :, 640:] = jnp.where(top, squares, 0.0)
    second.wait()
    for step in range(6, PANELS):
        block = block_of(step)
        lanes = slice((step - 6) * LANES, (step - 5) * LANES)
        partial[1, 0, :, lanes] = block[:64]
        partial[1, 1, :, lanes] = block[64:]
    picked = rows_dot(chosen[0], landed_b[3]) + rows_dot(chosen[1], landed_b[4])
    for part in range(4):
        lanes = slice(384 + (part % 2) * LANES, 384 + (part % 2 + 1) * LANES)
        partial[1, part // 2, :, lanes] = picked[part * 64 : part * 64 + 64]
    reduce_begin(1)
    reduce_end(0)
    a0, a1, a2, a3 = [Strip(0, shift, shift % 2 == 1) for shift in (0, 1, 3, 2)]
    b0, b1, b2, b3 = [Strip(1, shift, shift % 2 == 1) for shift in (0, 1, 3, 2)]
    a0.begin()
    reduce_end(1)
    a1.begin(), a2.begin(), a3.begin()
    a0.middle(), a1.middle(), a2.middle(), b0.begin(), a3.middle()
    b1.begin(), b2.begin(), b3.begin()
    a0.forward(), a1.forward(), a2.forward(), a3.forward()
    b0.middle(), b1.middle(), b2.middle(), b3.middle()
    a0.finish(), a1.finish(), a2.finish(), a3.finish()
    b0.forward(), b1.forward(), b2.forward(), b3.forward()
    b0.finish(), b1.finish(), b2.finish(), b3.finish()
    for strip in (a0, a1, a2, a3, b0, b1, b2, b3):
        strip.last()
    for g in range(2):
        bytes_of(terms.at[g, pl.ds(1, 15)], send_back.at[g], recv_back.at[g, 0]).wait_send()

    def blocks(i, low, high):
        return everything[i // 4, (i // 2) % 2, i % 2, :, :, :, low:high].reshape(256, high - low)

    for chip in range(16):
        lanes = slice(chip * LANES, (chip + 1) * LANES)
        parts = everything[chip // 8, (chip // 4) % 2, (chip // 2) % 2, chip % 2, 0, 0:16, DIAG:].astype(F32)
        mean = (parts[0:1] + parts[1:2] + parts[2:3]) / sample_total
        inverse = 1.0 / jnp.sqrt(mean + EPSILON)
        scale[0:1, lanes] = inverse
        extra[0:1, lanes] = inverse * mean * inverse - 1.0
        for part in range(2):
            source = slice(GRAM + part * LANES, GRAM + (part + 1) * LANES)
            start[part * 64 : part * 64 + 64, lanes] = everything[chip // 8, (chip // 4) % 2, (chip // 2) % 2, chip % 2, core, :, source].astype(F32) * inverse
        start[128:, lanes] = pool[:, lanes].astype(F32) * inverse
    for pair in range(4):
        for side in range(2):
            span = slice(side * LANES, (side + 1) * LANES)
            others = slice((1 - side) * LANES, (2 - side) * LANES)
            corner[pair, span, span] = blocks(pair, GRAM - LANES, GRAM)[span]
            corner[pair, others, span] = blocks(pair + 4, GRAM - LANES, GRAM)[span].astype(F32).T.astype(BF16)
    held[...] = start[...] * (1.0 / 16.0)

    @pl.loop(0, 4)
    def _(turn):
        factor = jnp.where(turn == 0, -0.3125, jnp.where(turn == 1, 0.375, jnp.where(turn == 2, -0.5, 1.0)))
        for j in range(8):
            lanes = slice(j * 256, (j + 1) * 256)
            scaled = (held[:, lanes] * scale[0:1, lanes]).astype(BF16)
            ready[:, lanes] = scaled
            if j < 3:
                ready[:, 2048 + j * 256 : 2048 + (j + 1) * 256] = scaled
        for j in range(8):
            lanes = slice(j * 256, (j + 1) * 256)
            out = lanes_dot(ready[:, (j + 1) * 256 : (j + 4) * 256], blocks(j, 256, 1024))
            for d in range(4):
                i = (j - d) % 8
                out += jnp.dot(
                    ready[:, i * 256 : (i + 1) * 256], blocks(i, d * 256, (d + 1) * 256), preferred_element_type=F32
                )
            if j >= 4:
                out += jnp.dot(ready[:, (j - 4) * 256 : (j - 3) * 256], corner[j - 4], preferred_element_type=F32)
            else:
                out += lanes_dot(ready[:, (j + 4) * 256 : (j + 5) * 256], corner[j])
            held[:, lanes] = (
                out * (scale[0:1, lanes] * (1.0 / sample_total))
                + held[:, lanes] * extra[0:1, lanes]
                + factor * start[:, lanes]
            )

    whitened[...] = held[...].astype(BF16)
    swap = remote(whitened.at[pl.ds(0, 128)], twin_rows, core_send.at[2], core_recv.at[2], twin)
    wide = whitened[128:].astype(F32)
    squares = wide * wide
    ones = jnp.ones((8, LANES), BF16)
    row_norms = jnp.zeros((8, 64), F32)
    for chip in range(16):
        part = squares[:, chip * LANES : (chip + 1) * LANES]
        for _ in range(3):
            piece = part.astype(BF16)
            row_norms += lanes_dot(ones, piece)
            part -= piece.astype(F32)

    def closest(centre_rows):
        wide = centre_rows.astype(F32)
        norms = jnp.sum(wide * wide, axis=1, keepdims=True)
        squared = row_norms[0:1] + norms - 2.0 * lanes_dot(centre_rows, whitened[128:])
        return jnp.min(jnp.maximum(squared, 0.0), axis=0, keepdims=True)

    best = closest(whitened[0:128])
    swap.wait()
    best = jnp.minimum(best, closest(twin_rows[...]))
    nearest[...] = best / (2.0 * 16 * LANES)


VMEM = pl.BlockSpec(memory_space=pltpu.VMEM)
HBM = pl.BlockSpec(memory_space=pltpu.HBM)
DMA = pltpu.SemaphoreType.DMA
LIMIT = 56 * 1024 * 1024


def per_device(sample, pool, old_min, centers):
    width = sample.shape[1]
    sample_total = sample.shape[0] * lax.axis_size("dp") * lax.axis_size("feat")
    nearest = pl.pallas_call(
        lambda *refs: update_kernel(float(sample_total), *refs),
        out_shape=jax.ShapeDtypeStruct((1, pool.shape[0]), F32),
        in_specs=[HBM, HBM, VMEM],
        out_specs=VMEM,
        scratch_shapes=[
            pltpu.VMEM(sample.shape, BF16),
            pltpu.VMEM(pool.shape, BF16),
            pltpu.VMEM((16, 6, 32, LANES), BF16),
            pltpu.VMEM((16, 5, 32, LANES), BF16),
            pltpu.VMEM((6, 512, LANES), BF16),
            pltpu.VMEM((5, 512, LANES), BF16),
            pltpu.VMEM((2, 2, 64, 768), F32),
            pltpu.VMEM((2, 64, 768), F32),
            pltpu.VMEM((2, 64, 768), BF16),
            pltpu.VMEM((2, 16, 8, 384), BF16),
            pltpu.VMEM((2, 8, 384), BF16),
            pltpu.VMEM((2, 2, 2, 2, 2, 64, SLAB), BF16),
            pltpu.VMEM((192, width), F32),
            pltpu.VMEM((192, width), F32),
            pltpu.VMEM((192, width + 768), BF16),
            pltpu.VMEM((4, 256, 256), BF16),
            pltpu.VMEM((8, width), F32),
            pltpu.VMEM((8, width), F32),
            pltpu.VMEM((192, width), BF16),
            pltpu.VMEM((128, width), BF16),
            DMA((8,)),
            DMA((2,)),
            DMA((2,)),
            DMA((3,)),
            DMA((3,)),
            DMA((2,)),
            DMA((2,)),
            DMA((2,)),
            DMA((2, 4)),
            DMA((8, 2)),
            DMA((8, 9)),
        ],
        compiler_params=pltpu.CompilerParams(collective_id=0, has_side_effects=True, vmem_limit_bytes=LIMIT),
    )(sample, pool, centers.reshape(1, 256))
    return jnp.minimum(old_min, nearest.reshape(old_min.shape))


def solution(mesh):
    return jax.shard_map(
        per_device,
        mesh=mesh,
        in_specs=(P(("dp", "feat"), None), P(("dp", "feat"), None), P(("dp", "feat")), P()),
        out_specs=P(("dp", "feat")),
        check_vma=False,
    )
```

```python
import jax
import jax.numpy as jnp
from jax import lax
from jax.experimental import pallas as pl
from jax.experimental.pallas import tpu as pltpu
from jax.sharding import PartitionSpec as P

EPSILON = 1e-06
MESH = pl.DeviceIdType.MESH
F32 = jnp.float32
BF16 = jnp.bfloat16
LANES = 128
PANELS = 9
SLAB = 1536
GRAM = LANES
CENTRE = GRAM + PANELS * LANES
GROUPS = ((0, 768), (768, 512), (1280, 256))
PARTS = ((0, 5), (5, 4), (9, 2))


def position():
    dp = lax.axis_index("dp")
    feat = lax.axis_index("feat")
    x, y = feat // 8, dp % 4
    z = (dp // 4) * 4 + (feat // 2) % 4
    return x, y, z, feat % 2


def device(x, y, z, core):
    return ((z // 4) * 4 + y, x * 8 + (z % 4) * 2 + core)


def remote(src, dst, send, recv, where):
    copy = pltpu.make_async_remote_copy(
        src_ref=src, dst_ref=dst, send_sem=send, recv_sem=recv, device_id=where, device_id_type=MESH
    )
    copy.start()
    return copy


def column_panels(chip):
    pair, half = chip // 2, chip % 2
    last = half if pair < 4 else 1 - half
    return [(2 * pair + step) % 16 for step in range(8)] + [(2 * pair + 8 + last) % 16]


def in_three(total, count):
    high = total.astype(BF16).astype(F32)
    middle = (total - high).astype(BF16).astype(F32)
    low = total - high - middle
    rows = lax.broadcasted_iota(jnp.int32, (count, LANES), 0)
    return jnp.where(rows == 0, high, jnp.where(rows == 1, middle, jnp.where(rows == 2, low, 0.0)))


def rows_dot(left, right):
    return lax.dot_general(left, right, (((0,), (0,)), ((), ())), preferred_element_type=F32)


def lanes_dot(left, right):
    return lax.dot_general(left, right, (((1,), (1,)), ((), ())), preferred_element_type=F32)


def update_kernel(
    sample_total, sample_in, pool_in, centers, nearest, sample, pool, parcels, landed, partial, other, mine,
    terms_a, terms_b, terms_c, chunk_a, chunk_b, chunk_c, everything, start, held, ready, corner, scale, extra, whitened, twin_rows, local, plane_send, plane_recv,
    core_send, core_recv, send, recv, send_back, recv_back, strip_send, strip_recv,
):
    x, y, z, core = position()
    here = x * 4 + y
    twin = device(x, y, z, 1 - core)
    column = [(z + o) % 16 for o in range(16)]
    far_first = [8] + [o for d in range(7, 0, -1) for o in (d, 16 - d)]
    offsets = [(dx, dy) for dx in range(4) for dy in range(4) if dx or dy]
    loads = [
        pltpu.make_async_copy(sample_in, sample, local.at[0]),
        pltpu.make_async_copy(pool_in, pool, local.at[1]),
    ]
    for copy in loads:
        copy.start()
    barrier = pltpu.get_barrier_semaphore()
    partners = [device(x, y, column[o], core) for o in far_first]
    partners += [device((x + dx) % 4, (y + dy) % 4, z, core) for dx, dy in offsets] + [twin]
    for partner in partners:
        pl.semaphore_signal(barrier, inc=1, device_id=partner, device_id_type=MESH)

    for copy in loads:
        copy.wait()
    for chip in range(16):
        for step, panel in enumerate(column_panels(chip)):
            parcels[chip, step] = sample[:, panel * LANES : (panel + 1) * LANES]
        for part in range(2):
            parcels[chip, PANELS + part] = pool[part * 32 : part * 32 + 32, chip * LANES : (chip + 1) * LANES]
    pl.semaphore_wait(barrier, len(partners))

    def bytes_of(ref, send_sem, recv_sem):
        return pltpu.make_async_remote_copy(
            src_ref=ref, dst_ref=ref, send_sem=send_sem, recv_sem=recv_sem, device_id=twin, device_id_type=MESH
        )

    rows = pl.ds(pl.multiple_of(here * 32, 32), 32)
    terms, chunk = [terms_a, terms_b, terms_c], [chunk_a, chunk_b, chunk_c]

    def exchange(g):
        panels = pl.ds(*PARTS[g])
        for dx, dy in offsets:
            to_x, to_y = (x + dx) % 4, (y + dy) % 4
            remote(
                parcels.at[to_x * 4 + to_y, panels],
                landed.at[panels, rows, :],
                plane_send.at[g],
                plane_recv.at[g],
                device(to_x, to_y, z, core),
            )
        own = pltpu.make_async_copy(parcels.at[here, panels], landed.at[panels, rows, :], local.at[2 + g])
        own.start()
        own.wait()
        return bytes_of(landed.at[panels, pl.ds(0, 480), :], plane_send.at[g], plane_recv.at[g])

    half = y % 2

    def fill_moments(first, count):
        for step in range(first, first + count):
            block = rows_dot(landed[half], landed[step])
            if step < 2:
                down = lax.broadcasted_iota(jnp.int32, block.shape, 0)
                along = lax.broadcasted_iota(jnp.int32, block.shape, 1)
                block = jnp.where((down == along) & (half == step), 0.0, block)
            lanes = slice(GRAM + step * LANES, GRAM + (step + 1) * LANES)
            partial[0, :, lanes] = block[:64]
            partial[1, :, lanes] = block[64:]

    def tiles(ref, k, width):
        return ref.at[pl.ds(pl.multiple_of((k // 2) * 8, 8), 8), pl.ds(pl.multiple_of((k % 2) * width, width), width)]

    def group(ref, g):
        return ref.at[:, pl.ds(*GROUPS[g])]

    def reduce_begin(g):
        low, wide = GROUPS[g]
        lanes = pl.ds(low, wide)
        remote(partial.at[1 - core, :, lanes], other.at[:, lanes], core_send.at[g], core_recv.at[g], twin).wait()
        if g == 0:
            mine[:, LANES:wide] = (partial[core, :, LANES:wide] + other[:, LANES:wide]).astype(BF16)
            squares = partial[core, 0:1, :LANES] + other[0:1, :LANES]
            mine[0:16, :LANES] = in_three(squares, 16).astype(BF16)
            mine[16:64, :LANES] = jnp.zeros((48, LANES), BF16)
        else:
            mine[:, lanes] = (partial[core, :, lanes] + other[:, lanes]).astype(BF16)
        own = pltpu.make_async_copy(tiles(group(mine, g), z, wide // 2), terms[g].at[0], local.at[5 + g])
        own.start()
        for o in far_first:
            remote(
                tiles(group(mine, g), column[o], wide // 2), terms[g].at[o], send.at[g], recv.at[g], device(x, y, column[o], core)
            )
        own.wait()

    def reduce_end(g):
        width = GROUPS[g][1] // 2
        bytes_of(terms[g].at[pl.ds(1, 15)], send.at[g], recv.at[g]).wait()
        total = terms[g][0].astype(F32)
        for o in range(1, 16):
            total += terms[g][o].astype(F32)
        if g == 0:
            squares = total[0:1, :LANES] + total[1:2, :LANES] + total[2:3, :LANES]
            chunk[g][:, :LANES] = jnp.where(z == 0, in_three(squares, 8), total[:, :LANES]).astype(BF16)
            chunk[g][:, LANES:] = total[:, LANES:].astype(BF16)
        else:
            chunk[g][...] = total.astype(BF16)
        place = tiles(group(everything.at[x // 2, x % 2, y // 2, y % 2, core], g), z, width)
        own = pltpu.make_async_copy(chunk[g], place, local.at[8 + g])
        own.start()
        zone_of = z // 4 if g == 0 else 0
        for o in far_first:
            remote(chunk[g], place, send_back.at[g], recv_back.at[g, zone_of], device(x, y, column[o], core))
        own.wait()

    zone = z // 4

    class Strip:
        def __init__(self, group, shift, flip):
            self.group, self.shift, self.flip = group, shift, flip
            count = 16 if group == 0 else 32
            self.a = (zone + shift) % 4 if group == 0 else shift
            self.place = (pl.ds(pl.multiple_of(self.a * count, count), count), pl.ds(*GROUPS[group]))
            p, q = (y, x) if flip else (x, y)
            self.p = [(p + 4 - d) % 4 for d in range(4)]
            self.q = [(q + 4 - d) % 4 for d in range(4)]
            number = (0, 4, 6)[group] + shift
            self.sent = [strip_send.at[number, n] for n in range(2)]
            self.got = [strip_recv.at[number, n] for n in range(9)]

        def where(self, p, q):
            return device(q, p, z, core) if self.flip else device(p, q, z, core)

        def at(self, p, q):
            first, second = (q, p) if self.flip else (p, q)
            return everything.at[first + second + (core,) + self.place]

        def piece(self, p, q):
            return self.at((p // 2, p % 2), (q // 2, q % 2))

        def pair(self, parity, q):
            return self.at((slice(None), parity), (q // 2, q % 2))

        def line(self, q):
            return self.at((slice(None), slice(None)), (q // 2, q % 2))

        def across(self, n):
            piece = self.piece(self.p[n], self.q[0])
            remote(piece, piece, self.sent[0], self.got[3 + n % 2], self.where(self.p[0], self.q[3]))
            remote(piece, piece, self.sent[0], self.got[5 + n % 2], self.where(self.p[0], self.q[1]))

        def twins(self, d):
            line = self.line(self.q[d])
            remote(line, line, self.sent[1], self.got[8], twin)

        def begin(self):
            if self.group == 0:
                ref = terms_a.at[pl.ds(0, 3)] if self.shift == 0 else self.piece(self.p[0], self.q[0])
                bytes_of(ref, send_back.at[0], recv_back.at[0, self.a]).wait_recv()
            elif self.shift == 0:
                bytes_of(terms[self.group].at[pl.ds(1, 15)], send_back.at[self.group], recv_back.at[self.group, 0]).wait_recv()
            piece = self.piece(self.p[0], self.q[0])
            for d in (2, 1, 3):
                remote(piece, piece, self.sent[0], self.got[d - 1], self.where(self.p[4 - d], self.q[0]))
            self.across(0)

        def middle(self):
            for d in (1, 3, 2):
                bytes_of(self.piece(self.p[d], self.q[0]), self.sent[0], self.got[d - 1]).wait_recv()
                self.across(d)
            self.twins(0)

        def forward(self):
            same, other = self.p[0] % 2, 1 - self.p[0] % 2
            up, down = self.pair(same, self.q[1]), self.pair(other, self.q[3])
            bytes_of(up, self.sent[0], self.got[3]).wait_recv()
            remote(up, up, self.sent[0], self.got[7], self.where(self.p[0], self.q[3]))
            bytes_of(down, self.sent[0], self.got[6]).wait_recv()
            remote(down, down, self.sent[0], self.got[7], self.where(self.p[0], self.q[1]))
            bytes_of(self.pair(other, self.q[1]), self.sent[0], self.got[4]).wait_recv()
            self.twins(1)
            bytes_of(self.pair(same, self.q[3]), self.sent[0], self.got[5]).wait_recv()
            self.twins(3)

        def finish(self):
            bytes_of(self.line(self.q[2]), self.sent[0], self.got[7]).wait_recv()
            self.twins(2)

        def last(self):
            every = slice(None)
            whole = everything.at[(every, every, every, every, 1 - core) + self.place]
            bytes_of(whole, self.sent[1], self.got[8]).wait()
            bytes_of(landed.at[pl.ds(0, (3, 4, 2)[self.group]), pl.ds(0, 480), :], self.sent[0], self.got[0]).wait_send()

    first = exchange(0)
    row = lax.broadcasted_iota(jnp.int32, (512, 256), 0)
    owner = ((z // 4) * 4 + ((row >> 5) & 3)) * 32 + (row >> 7) * 8 + (z % 4) * 2 + core
    row_id = owner * 64 + (row & 31)
    chosen = [jnp.where(row_id + part * 32 == centers[...], 1.0, 0.0).astype(BF16) for part in range(2)]
    first.wait_send()
    second = exchange(1)
    first.wait_recv()
    fill_moments(*PARTS[0])
    wide = landed[half].astype(F32)
    squares = jnp.sum(wide * wide, axis=0, keepdims=True)
    top = lax.broadcasted_iota(jnp.int32, (64, LANES), 0) == 0
    for side in range(2):
        partial[side, :, :LANES] = jnp.where(top, squares, 0.0)
    reduce_begin(0)
    second.wait_send()
    third = exchange(2)
    second.wait_recv()
    fill_moments(*PARTS[1])
    reduce_begin(1)
    third.wait()
    picked = rows_dot(chosen[0], landed[PANELS]) + rows_dot(chosen[1], landed[PANELS + 1])
    for part in range(4):
        lanes = slice(CENTRE + (part % 2) * LANES, CENTRE + (part % 2 + 1) * LANES)
        partial[part // 2, :, lanes] = picked[part * 64 : part * 64 + 64]
    reduce_begin(2)
    reduce_end(0)
    strips_a = [Strip(0, shift, shift % 2 == 1) for shift in (0, 1, 3, 2)]
    strips_b = [Strip(1, shift, shift == 1) for shift in (0, 1)]
    strips_c = [Strip(2, shift, shift == 1) for shift in (0, 1)]

    def every(strips, what):
        for strip in strips:
            getattr(strip, what)()

    strips_a[0].begin()
    reduce_end(1)
    every(strips_a[1:], "begin")
    reduce_end(2)
    every(strips_a, "middle")
    every(strips_b, "begin")
    every(strips_a, "forward")
    every(strips_c, "begin")
    every(strips_b, "middle")
    every(strips_a, "finish")
    every(strips_c, "middle")
    every(strips_b, "forward")
    every(strips_c, "forward")
    every(strips_b, "finish")
    every(strips_c, "finish")
    every(strips_a + strips_b + strips_c, "last")
    for g in range(3):
        bytes_of(terms[g].at[pl.ds(1, 15)], send_back.at[g], recv_back.at[g, 0]).wait_send()

    def blocks(i, low, high):
        return everything[i // 4, (i // 2) % 2, i % 2, :, :, :, low:high].reshape(256, high - low)

    for chip in range(16):
        lanes = slice(chip * LANES, (chip + 1) * LANES)
        parts = everything[chip // 8, (chip // 4) % 2, (chip // 2) % 2, chip % 2, 0, 0:16, :LANES].astype(F32)
        mean = (parts[0:1] + parts[1:2] + parts[2:3]) / sample_total
        inverse = 1.0 / jnp.sqrt(mean + EPSILON)
        scale[0:1, lanes] = inverse
        extra[0:1, lanes] = inverse * mean * inverse - 1.0
        for part in range(2):
            source = slice(CENTRE + part * LANES, CENTRE + (part + 1) * LANES)
            start[part * 64 : part * 64 + 64, lanes] = everything[chip // 8, (chip // 4) % 2, (chip // 2) % 2, chip % 2, core, :, source].astype(F32) * inverse
        start[128:, lanes] = pool[:, lanes].astype(F32) * inverse
    for pair in range(4):
        for side in range(2):
            span = slice(side * LANES, (side + 1) * LANES)
            others = slice((1 - side) * LANES, (2 - side) * LANES)
            corner[pair, span, span] = blocks(pair, CENTRE - LANES, CENTRE)[span]
            corner[pair, others, span] = blocks(pair + 4, CENTRE - LANES, CENTRE)[span].astype(F32).T.astype(BF16)
    held[...] = start[...] * (1.0 / 16.0)

    @pl.loop(0, 4)
    def _(turn):
        factor = jnp.where(turn == 0, -0.3125, jnp.where(turn == 1, 0.375, jnp.where(turn == 2, -0.5, 1.0)))
        for j in range(8):
            lanes = slice(j * 256, (j + 1) * 256)
            scaled = (held[:, lanes] * scale[0:1, lanes]).astype(BF16)
            ready[:, lanes] = scaled
            if j < 3:
                ready[:, 2048 + j * 256 : 2048 + (j + 1) * 256] = scaled
        for j in range(8):
            lanes = slice(j * 256, (j + 1) * 256)
            out = lanes_dot(ready[:, (j + 1) * 256 : (j + 4) * 256], blocks(j, GRAM + 256, GRAM + 1024))
            for d in range(4):
                i = (j - d) % 8
                out += jnp.dot(
                    ready[:, i * 256 : (i + 1) * 256], blocks(i, GRAM + d * 256, GRAM + (d + 1) * 256), preferred_element_type=F32
                )
            if j >= 4:
                out += jnp.dot(ready[:, (j - 4) * 256 : (j - 3) * 256], corner[j - 4], preferred_element_type=F32)
            else:
                out += lanes_dot(ready[:, (j + 4) * 256 : (j + 5) * 256], corner[j])
            held[:, lanes] = (
                out * (scale[0:1, lanes] * (1.0 / sample_total))
                + held[:, lanes] * extra[0:1, lanes]
                + factor * start[:, lanes]
            )

    whitened[...] = held[...].astype(BF16)
    swap = remote(whitened.at[pl.ds(0, 128)], twin_rows, core_send.at[3], core_recv.at[3], twin)
    wide = whitened[128:].astype(F32)
    squares = wide * wide
    ones = jnp.ones((8, LANES), BF16)
    row_norms = jnp.zeros((8, 64), F32)
    for chip in range(16):
        part = squares[:, chip * LANES : (chip + 1) * LANES]
        for _ in range(3):
            piece = part.astype(BF16)
            row_norms += lanes_dot(ones, piece)
            part -= piece.astype(F32)

    def closest(centre_rows):
        wide = centre_rows.astype(F32)
        norms = jnp.sum(wide * wide, axis=1, keepdims=True)
        squared = row_norms[0:1] + norms - 2.0 * lanes_dot(centre_rows, whitened[128:])
        return jnp.min(jnp.maximum(squared, 0.0), axis=0, keepdims=True)

    best = closest(whitened[0:128])
    swap.wait()
    best = jnp.minimum(best, closest(twin_rows[...]))
    nearest[...] = best / (2.0 * 16 * LANES)


VMEM = pl.BlockSpec(memory_space=pltpu.VMEM)
HBM = pl.BlockSpec(memory_space=pltpu.HBM)
DMA = pltpu.SemaphoreType.DMA
LIMIT = 56 * 1024 * 1024


def per_device(sample, pool, old_min, centers):
    width = sample.shape[1]
    sample_total = sample.shape[0] * lax.axis_size("dp") * lax.axis_size("feat")
    nearest = pl.pallas_call(
        lambda *refs: update_kernel(float(sample_total), *refs),
        out_shape=jax.ShapeDtypeStruct((1, pool.shape[0]), F32),
        in_specs=[HBM, HBM, VMEM],
        out_specs=VMEM,
        scratch_shapes=[
            pltpu.VMEM(sample.shape, BF16),
            pltpu.VMEM(pool.shape, BF16),
            pltpu.VMEM((16, PANELS + 2, 32, LANES), BF16),
            pltpu.VMEM((PANELS + 2, 512, LANES), BF16),
            pltpu.VMEM((2, 64, SLAB), F32),
            pltpu.VMEM((64, SLAB), F32),
            pltpu.VMEM((64, SLAB), BF16),
            *[pltpu.VMEM((16, 8, wide // 2), BF16) for _, wide in GROUPS],
            *[pltpu.VMEM((8, wide // 2), BF16) for _, wide in GROUPS],
            pltpu.VMEM((2, 2, 2, 2, 2, 64, SLAB), BF16),
            pltpu.VMEM((192, width), F32),
            pltpu.VMEM((192, width), F32),
            pltpu.VMEM((192, width + 768), BF16),
            pltpu.VMEM((4, 256, 256), BF16),
            pltpu.VMEM((8, width), F32),
            pltpu.VMEM((8, width), F32),
            pltpu.VMEM((192, width), BF16),
            pltpu.VMEM((128, width), BF16),
            DMA((11,)),
            DMA((3,)),
            DMA((3,)),
            DMA((4,)),
            DMA((4,)),
            DMA((3,)),
            DMA((3,)),
            DMA((3,)),
            DMA((3, 4)),
            DMA((8, 2)),
            DMA((8, 9)),
        ],
        compiler_params=pltpu.CompilerParams(collective_id=0, has_side_effects=True, vmem_limit_bytes=LIMIT),
    )(sample, pool, centers.reshape(1, 256))
    return jnp.minimum(old_min, nearest.reshape(old_min.shape))


def solution(mesh):
    return jax.shard_map(
        per_device,
        mesh=mesh,
        in_specs=(P(("dp", "feat"), None), P(("dp", "feat"), None), P(("dp", "feat")), P()),
        out_specs=P(("dp", "feat")),
        check_vma=False,
    )
```

```python
import jax
import jax.numpy as jnp
from jax import lax
from jax.experimental import pallas as pl
from jax.experimental.pallas import tpu as pltpu
from jax.sharding import PartitionSpec as P

EPSILON = 1e-06
MESH = pl.DeviceIdType.MESH
F32 = jnp.float32
BF16 = jnp.bfloat16
LANES = 128
PANELS = 9
SLAB = 1536
GRAM = LANES
CENTRE = GRAM + PANELS * LANES
GROUPS = ((0, 768), (768, 512), (1280, 256))
PARTS = ((0, 5), (5, 4), (9, 2))


def position():
    dp = lax.axis_index("dp")
    feat = lax.axis_index("feat")
    x, y = feat // 8, dp % 4
    z = (dp // 4) * 4 + (feat // 2) % 4
    return x, y, z, feat % 2


def device(x, y, z, core):
    return ((z // 4) * 4 + y, x * 8 + (z % 4) * 2 + core)


def remote(src, dst, send, recv, where):
    copy = pltpu.make_async_remote_copy(
        src_ref=src, dst_ref=dst, send_sem=send, recv_sem=recv, device_id=where, device_id_type=MESH
    )
    copy.start()
    return copy


def column_panels(chip):
    pair, half = chip // 2, chip % 2
    last = half if pair < 4 else 1 - half
    return [(2 * pair + step) % 16 for step in range(8)] + [(2 * pair + 8 + last) % 16]


def in_three(total, count):
    high = total.astype(BF16).astype(F32)
    middle = (total - high).astype(BF16).astype(F32)
    low = total - high - middle
    rows = lax.broadcasted_iota(jnp.int32, (count, LANES), 0)
    return jnp.where(rows == 0, high, jnp.where(rows == 1, middle, jnp.where(rows == 2, low, 0.0)))


def rows_dot(left, right):
    return lax.dot_general(left, right, (((0,), (0,)), ((), ())), preferred_element_type=F32)


def lanes_dot(left, right):
    return lax.dot_general(left, right, (((1,), (1,)), ((), ())), preferred_element_type=F32)


def update_kernel(
    sample_total, sample_in, pool_in, centers, nearest, sample, pool, parcels, landed, partial, other, mine,
    terms_a, terms_b, terms_c, chunk_a, chunk_b, chunk_c, everything, start, held, ready, corner, scale, extra, whitened, twin_rows, local, plane_send, plane_recv,
    core_send, core_recv, send, recv, send_back, recv_back, strip_send, strip_recv,
):
    x, y, z, core = position()
    here = x * 4 + y
    twin = device(x, y, z, 1 - core)
    column = [(z + o) % 16 for o in range(16)]
    far_first = [8] + [o for d in range(7, 0, -1) for o in (d, 16 - d)]
    offsets = [(dx, dy) for dx in range(4) for dy in range(4) if dx or dy]
    loads = [
        pltpu.make_async_copy(sample_in, sample, local.at[0]),
        pltpu.make_async_copy(pool_in, pool, local.at[1]),
    ]
    for copy in loads:
        copy.start()
    barrier = pltpu.get_barrier_semaphore()
    partners = [device(x, y, column[o], core) for o in far_first]
    partners += [device((x + dx) % 4, (y + dy) % 4, z, core) for dx, dy in offsets] + [twin]
    for partner in partners:
        pl.semaphore_signal(barrier, inc=1, device_id=partner, device_id_type=MESH)

    for copy in loads:
        copy.wait()
    for chip in range(16):
        for step, panel in enumerate(column_panels(chip)):
            parcels[chip, step] = sample[:, panel * LANES : (panel + 1) * LANES]
        for part in range(2):
            parcels[chip, PANELS + part] = pool[part * 32 : part * 32 + 32, chip * LANES : (chip + 1) * LANES]
    pl.semaphore_wait(barrier, len(partners))

    def bytes_of(ref, send_sem, recv_sem):
        return pltpu.make_async_remote_copy(
            src_ref=ref, dst_ref=ref, send_sem=send_sem, recv_sem=recv_sem, device_id=twin, device_id_type=MESH
        )

    rows = pl.ds(pl.multiple_of(here * 32, 32), 32)
    terms, chunk = [terms_a, terms_b, terms_c], [chunk_a, chunk_b, chunk_c]

    def exchange(g):
        panels = pl.ds(*PARTS[g])
        for dx, dy in offsets:
            to_x, to_y = (x + dx) % 4, (y + dy) % 4
            remote(
                parcels.at[to_x * 4 + to_y, panels],
                landed.at[panels, rows, :],
                plane_send.at[g],
                plane_recv.at[g],
                device(to_x, to_y, z, core),
            )
        own = pltpu.make_async_copy(parcels.at[here, panels], landed.at[panels, rows, :], local.at[2 + g])
        own.start()
        own.wait()
        return bytes_of(landed.at[panels, pl.ds(0, 480), :], plane_send.at[g], plane_recv.at[g])

    half = y % 2

    def fill_moments(first, count):
        for step in range(first, first + count):
            block = rows_dot(landed[half], landed[step])
            if step < 2:
                down = lax.broadcasted_iota(jnp.int32, block.shape, 0)
                along = lax.broadcasted_iota(jnp.int32, block.shape, 1)
                block = jnp.where((down == along) & (half == step), 0.0, block)
            lanes = slice(GRAM + step * LANES, GRAM + (step + 1) * LANES)
            partial[0, :, lanes] = block[:64]
            partial[1, :, lanes] = block[64:]

    def tiles(ref, k, width):
        return ref.at[pl.ds(pl.multiple_of((k // 2) * 8, 8), 8), pl.ds(pl.multiple_of((k % 2) * width, width), width)]

    def group(ref, g):
        return ref.at[:, pl.ds(*GROUPS[g])]

    def reduce_begin(g):
        low, wide = GROUPS[g]
        lanes = pl.ds(low, wide)
        remote(partial.at[1 - core, :, lanes], other.at[:, lanes], core_send.at[g], core_recv.at[g], twin).wait()
        if g == 0:
            mine[:, LANES:wide] = (partial[core, :, LANES:wide] + other[:, LANES:wide]).astype(BF16)
            squares = partial[core, 0:1, :LANES] + other[0:1, :LANES]
            mine[0:16, :LANES] = in_three(squares, 16).astype(BF16)
            mine[16:64, :LANES] = jnp.zeros((48, LANES), BF16)
        else:
            mine[:, lanes] = (partial[core, :, lanes] + other[:, lanes]).astype(BF16)
        own = pltpu.make_async_copy(tiles(group(mine, g), z, wide // 2), terms[g].at[0], local.at[5 + g])
        own.start()
        for o in far_first:
            remote(
                tiles(group(mine, g), column[o], wide // 2), terms[g].at[o], send.at[g], recv.at[g], device(x, y, column[o], core)
            )
        own.wait()

    def reduce_end(g):
        width = GROUPS[g][1] // 2
        bytes_of(terms[g].at[pl.ds(1, 15)], send.at[g], recv.at[g]).wait()
        total = terms[g][0].astype(F32)
        for o in range(1, 16):
            total += terms[g][o].astype(F32)
        if g == 0:
            squares = total[0:1, :LANES] + total[1:2, :LANES] + total[2:3, :LANES]
            chunk[g][:, :LANES] = jnp.where(z == 0, in_three(squares, 8), total[:, :LANES]).astype(BF16)
            chunk[g][:, LANES:] = total[:, LANES:].astype(BF16)
        else:
            chunk[g][...] = total.astype(BF16)
        place = tiles(group(everything.at[x // 2, x % 2, y // 2, y % 2, core], g), z, width)
        own = pltpu.make_async_copy(chunk[g], place, local.at[8 + g])
        own.start()
        zone_of = z // 4 if g == 0 else 0
        for o in far_first:
            remote(chunk[g], place, send_back.at[g], recv_back.at[g, zone_of], device(x, y, column[o], core))
        own.wait()

    zone = z // 4

    class Strip:
        def __init__(self, group, shift, flip):
            self.group, self.shift, self.flip = group, shift, flip
            count = 16 if group == 0 else 32
            self.a = (zone + shift) % 4 if group == 0 else shift
            self.place = (pl.ds(pl.multiple_of(self.a * count, count), count), pl.ds(*GROUPS[group]))
            p, q = (y, x) if flip else (x, y)
            self.p = [(p + 4 - d) % 4 for d in range(4)]
            self.q = [(q + 4 - d) % 4 for d in range(4)]
            number = (0, 4, 6)[group] + shift
            self.sent = [strip_send.at[number, n] for n in range(2)]
            self.got = [strip_recv.at[number, n] for n in range(9)]

        def where(self, p, q):
            return device(q, p, z, core) if self.flip else device(p, q, z, core)

        def at(self, p, q):
            first, second = (q, p) if self.flip else (p, q)
            return everything.at[first + second + (core,) + self.place]

        def piece(self, p, q):
            return self.at((p // 2, p % 2), (q // 2, q % 2))

        def pair(self, parity, q):
            return self.at((slice(None), parity), (q // 2, q % 2))

        def line(self, q):
            return self.at((slice(None), slice(None)), (q // 2, q % 2))

        def across(self, n):
            piece = self.piece(self.p[n], self.q[0])
            remote(piece, piece, self.sent[0], self.got[3 + n % 2], self.where(self.p[0], self.q[3]))
            remote(piece, piece, self.sent[0], self.got[5 + n % 2], self.where(self.p[0], self.q[1]))

        def twins(self, d):
            line = self.line(self.q[d])
            remote(line, line, self.sent[1], self.got[8], twin)

        def begin(self):
            if self.group == 0:
                ref = terms_a.at[pl.ds(0, 3)] if self.shift == 0 else self.piece(self.p[0], self.q[0])
                bytes_of(ref, send_back.at[0], recv_back.at[0, self.a]).wait_recv()
            elif self.shift == 0:
                bytes_of(terms[self.group].at[pl.ds(1, 15)], send_back.at[self.group], recv_back.at[self.group, 0]).wait_recv()
            piece = self.piece(self.p[0], self.q[0])
            for d in (2, 1, 3):
                remote(piece, piece, self.sent[0], self.got[d - 1], self.where(self.p[4 - d], self.q[0]))
            self.across(0)

        def middle(self):
            for d in (1, 3, 2):
                bytes_of(self.piece(self.p[d], self.q[0]), self.sent[0], self.got[d - 1]).wait_recv()
                self.across(d)
            self.twins(0)

        def forward(self):
            same, other = self.p[0] % 2, 1 - self.p[0] % 2
            up, down = self.pair(same, self.q[1]), self.pair(other, self.q[3])
            bytes_of(up, self.sent[0], self.got[3]).wait_recv()
            remote(up, up, self.sent[0], self.got[7], self.where(self.p[0], self.q[3]))
            bytes_of(down, self.sent[0], self.got[6]).wait_recv()
            remote(down, down, self.sent[0], self.got[7], self.where(self.p[0], self.q[1]))
            bytes_of(self.pair(other, self.q[1]), self.sent[0], self.got[4]).wait_recv()
            self.twins(1)
            bytes_of(self.pair(same, self.q[3]), self.sent[0], self.got[5]).wait_recv()
            self.twins(3)

        def finish(self):
            bytes_of(self.line(self.q[2]), self.sent[0], self.got[7]).wait_recv()
            self.twins(2)

        def last(self):
            every = slice(None)
            whole = everything.at[(every, every, every, every, 1 - core) + self.place]
            bytes_of(whole, self.sent[1], self.got[8]).wait()
            bytes_of(landed.at[pl.ds(0, (3, 4, 2)[self.group]), pl.ds(0, 480), :], self.sent[0], self.got[0]).wait_send()

    first, second, third = exchange(0), exchange(1), exchange(2)
    row = lax.broadcasted_iota(jnp.int32, (512, 256), 0)
    owner = ((z // 4) * 4 + ((row >> 5) & 3)) * 32 + (row >> 7) * 8 + (z % 4) * 2 + core
    row_id = owner * 64 + (row & 31)
    chosen = [jnp.where(row_id + part * 32 == centers[...], 1.0, 0.0).astype(BF16) for part in range(2)]
    first.wait()
    fill_moments(*PARTS[0])
    wide = landed[half].astype(F32)
    squares = jnp.sum(wide * wide, axis=0, keepdims=True)
    top = lax.broadcasted_iota(jnp.int32, (64, LANES), 0) == 0
    for side in range(2):
        partial[side, :, :LANES] = jnp.where(top, squares, 0.0)
    reduce_begin(0)
    second.wait()
    fill_moments(*PARTS[1])
    reduce_begin(1)
    third.wait()
    picked = rows_dot(chosen[0], landed[PANELS]) + rows_dot(chosen[1], landed[PANELS + 1])
    for part in range(4):
        lanes = slice(CENTRE + (part % 2) * LANES, CENTRE + (part % 2 + 1) * LANES)
        partial[part // 2, :, lanes] = picked[part * 64 : part * 64 + 64]
    reduce_begin(2)
    reduce_end(0)
    strips_a = [Strip(0, shift, shift % 2 == 1) for shift in (0, 1, 3, 2)]
    strips_b = [Strip(1, shift, shift == 1) for shift in (0, 1)]
    strips_c = [Strip(2, shift, shift == 1) for shift in (0, 1)]

    def every(strips, what):
        for strip in strips:
            getattr(strip, what)()

    strips_a[0].begin()
    reduce_end(1)
    every(strips_a[1:], "begin")
    reduce_end(2)
    every(strips_a, "middle")
    every(strips_b, "begin")
    every(strips_a, "forward")
    every(strips_c, "begin")
    every(strips_b, "middle")
    every(strips_a, "finish")
    every(strips_c, "middle")
    every(strips_b, "forward")
    every(strips_c, "forward")
    every(strips_b, "finish")
    every(strips_c, "finish")
    every(strips_a + strips_b + strips_c, "last")
    for g in range(3):
        bytes_of(terms[g].at[pl.ds(1, 15)], send_back.at[g], recv_back.at[g, 0]).wait_send()

    def blocks(i, low, high):
        return everything[i // 4, (i // 2) % 2, i % 2, :, :, :, low:high].reshape(256, high - low)

    for chip in range(16):
        lanes = slice(chip * LANES, (chip + 1) * LANES)
        parts = everything[chip // 8, (chip // 4) % 2, (chip // 2) % 2, chip % 2, 0, 0:16, :LANES].astype(F32)
        mean = (parts[0:1] + parts[1:2] + parts[2:3]) / sample_total
        inverse = 1.0 / jnp.sqrt(mean + EPSILON)
        scale[0:1, lanes] = inverse
        extra[0:1, lanes] = inverse * mean * inverse - 1.0
        for part in range(2):
            source = slice(CENTRE + part * LANES, CENTRE + (part + 1) * LANES)
            start[part * 64 : part * 64 + 64, lanes] = everything[chip // 8, (chip // 4) % 2, (chip // 2) % 2, chip % 2, core, :, source].astype(F32) * inverse
        start[128:, lanes] = pool[:, lanes].astype(F32) * inverse
    for pair in range(4):
        for side in range(2):
            span = slice(side * LANES, (side + 1) * LANES)
            others = slice((1 - side) * LANES, (2 - side) * LANES)
            corner[pair, span, span] = blocks(pair, CENTRE - LANES, CENTRE)[span]
            corner[pair, others, span] = blocks(pair + 4, CENTRE - LANES, CENTRE)[span].astype(F32).T.astype(BF16)
    held[...] = start[...] * (1.0 / 16.0)

    @pl.loop(0, 4)
    def _(turn):
        factor = jnp.where(turn == 0, -0.3125, jnp.where(turn == 1, 0.375, jnp.where(turn == 2, -0.5, 1.0)))
        for j in range(8):
            lanes = slice(j * 256, (j + 1) * 256)
            scaled = (held[:, lanes] * scale[0:1, lanes]).astype(BF16)
            ready[:, lanes] = scaled
            if j < 3:
                ready[:, 2048 + j * 256 : 2048 + (j + 1) * 256] = scaled
        for j in range(8):
            lanes = slice(j * 256, (j + 1) * 256)
            out = lanes_dot(ready[:, (j + 1) * 256 : (j + 4) * 256], blocks(j, GRAM + 256, GRAM + 1024))
            for d in range(4):
                i = (j - d) % 8
                out += jnp.dot(
                    ready[:, i * 256 : (i + 1) * 256], blocks(i, GRAM + d * 256, GRAM + (d + 1) * 256), preferred_element_type=F32
                )
            if j >= 4:
                out += jnp.dot(ready[:, (j - 4) * 256 : (j - 3) * 256], corner[j - 4], preferred_element_type=F32)
            else:
                out += lanes_dot(ready[:, (j + 4) * 256 : (j + 5) * 256], corner[j])
            held[:, lanes] = (
                out * (scale[0:1, lanes] * (1.0 / sample_total))
                + held[:, lanes] * extra[0:1, lanes]
                + factor * start[:, lanes]
            )

    whitened[...] = held[...].astype(BF16)
    swap = remote(whitened.at[pl.ds(0, 128)], twin_rows, core_send.at[3], core_recv.at[3], twin)
    wide = whitened[128:].astype(F32)
    squares = wide * wide
    ones = jnp.ones((8, LANES), BF16)
    row_norms = jnp.zeros((8, 64), F32)
    for chip in range(16):
        part = squares[:, chip * LANES : (chip + 1) * LANES]
        for _ in range(3):
            piece = part.astype(BF16)
            row_norms += lanes_dot(ones, piece)
            part -= piece.astype(F32)

    def closest(centre_rows):
        wide = centre_rows.astype(F32)
        norms = jnp.sum(wide * wide, axis=1, keepdims=True)
        squared = row_norms[0:1] + norms - 2.0 * lanes_dot(centre_rows, whitened[128:])
        return jnp.min(jnp.maximum(squared, 0.0), axis=0, keepdims=True)

    best = closest(whitened[0:128])
    swap.wait()
    best = jnp.minimum(best, closest(twin_rows[...]))
    nearest[...] = best / (2.0 * 16 * LANES)


VMEM = pl.BlockSpec(memory_space=pltpu.VMEM)
HBM = pl.BlockSpec(memory_space=pltpu.HBM)
DMA = pltpu.SemaphoreType.DMA
LIMIT = 56 * 1024 * 1024


def per_device(sample, pool, old_min, centers):
    width = sample.shape[1]
    sample_total = sample.shape[0] * lax.axis_size("dp") * lax.axis_size("feat")
    nearest = pl.pallas_call(
        lambda *refs: update_kernel(float(sample_total), *refs),
        out_shape=jax.ShapeDtypeStruct((1, pool.shape[0]), F32),
        in_specs=[HBM, HBM, VMEM],
        out_specs=VMEM,
        scratch_shapes=[
            pltpu.VMEM(sample.shape, BF16),
            pltpu.VMEM(pool.shape, BF16),
            pltpu.VMEM((16, PANELS + 2, 32, LANES), BF16),
            pltpu.VMEM((PANELS + 2, 512, LANES), BF16),
            pltpu.VMEM((2, 64, SLAB), F32),
            pltpu.VMEM((64, SLAB), F32),
            pltpu.VMEM((64, SLAB), BF16),
            *[pltpu.VMEM((16, 8, wide // 2), BF16) for _, wide in GROUPS],
            *[pltpu.VMEM((8, wide // 2), BF16) for _, wide in GROUPS],
            pltpu.VMEM((2, 2, 2, 2, 2, 64, SLAB), BF16),
            pltpu.VMEM((192, width), F32),
            pltpu.VMEM((192, width), F32),
            pltpu.VMEM((192, width + 768), BF16),
            pltpu.VMEM((4, 256, 256), BF16),
            pltpu.VMEM((8, width), F32),
            pltpu.VMEM((8, width), F32),
            pltpu.VMEM((192, width), BF16),
            pltpu.VMEM((128, width), BF16),
            DMA((11,)),
            DMA((3,)),
            DMA((3,)),
            DMA((4,)),
            DMA((4,)),
            DMA((3,)),
            DMA((3,)),
            DMA((3,)),
            DMA((3, 4)),
            DMA((8, 2)),
            DMA((8, 9)),
        ],
        compiler_params=pltpu.CompilerParams(collective_id=0, has_side_effects=True, vmem_limit_bytes=LIMIT),
    )(sample, pool, centers.reshape(1, 256))
    return jnp.minimum(old_min, nearest.reshape(old_min.shape))


def solution(mesh):
    return jax.shard_map(
        per_device,
        mesh=mesh,
        in_specs=(P(("dp", "feat"), None), P(("dp", "feat"), None), P(("dp", "feat")), P()),
        out_specs=P(("dp", "feat")),
        check_vma=False,
    )
```
